32 devices in a mesh: gx: 4 (over z), gy: 8 (over y, x, core).
Axes of the slice: x: 2, y: 2, z: 4, core: 2. Of those that a mesh axis runs over, the one named last changes fastest.
Arguments:
- wind_u: float32 [8, 128, 512], P(None, 'gy', 'gx'), may hold values from -6 to 6
- wind_v: float32 [8, 128, 512], P(None, 'gy', 'gx'), may hold values from -6 to 6
- turbines: int32 [128, 512], P('gy', 'gx'), may hold values from 0 to 6
- rotor_level: int32 [128, 512], P('gy', 'gx'), may hold values from 0 to 5
- block_source: int32 [8, 3], replicated, may hold values from 0 to 7, as said below
- block_weight: float32 [8, 3, 16, 16], replicated, may hold values from 0.0052083335 to 0.041666668
- spectra: float32 [36, 36, 512, 128], P(None, None, ('gx', 'gy')), may hold values from 0.01 to 1
- sea_mask: int32 [512, 128], P(('gx', 'gy')), may hold values 0 or 1
Outputs:
- wind_u_next: float32 [8, 128, 512], P(None, 'gy', 'gx')
- wind_v_next: float32 [8, 128, 512], P(None, 'gy', 'gx')
- spectra_next: float32 [36, 36, 512, 128], P(None, None, ('gx', 'gy'))
The draws below stay inside these ranges and needn't reach their ends.
Inputs may be any that keep to these rules, and one draw needn't show every extreme that they name: `block_source`: every block appears in slot 0 of exactly one destination block; other slots name any block.
All inputs are finite; a program needn't handle non-finite values. No bound on the sum of `sea_mask` on one device may be relied on, other than what follows from the above.
Results may differ from the reference program's by a relative error of at most 0.000062.
Values sent between devices are 32-bit elements; how exact they have to be, the bound alone decides.
A program may use at most 128 MiB of HBM per device.

```python
import math
import jax
import jax.numpy as jnp
from jax import lax

FREQS = 36
DIRS = 36
LEV = 8
ROTOR = 3
SLOTS = 3
AY = 16
NLON = 512
NLAT = 128
BLOCKS = 8


def draw_block_source(key, part):
    first = jax.random.permutation(jax.random.fold_in(key, 11), BLOCKS).astype(jnp.int32)[:, None]
    others = jax.random.randint(jax.random.fold_in(key, 12), (BLOCKS, SLOTS - 1), 0, BLOCKS).astype(jnp.int32)
    return jnp.concatenate([first, others], axis=1)


def set_ends(result, rng, smallest, largest):
    extent = result.shape
    index_at = [jax.random.randint(jax.random.fold_in(rng, axis), (), 0, extent[axis]) for axis in range(len(extent))]
    result = result.at[tuple(index_at)].set(smallest)
    longest = extent.index(max(extent))
    index_at[longest] = (index_at[longest] + 1) % extent[longest]
    return result.at[tuple(index_at)].set(largest)


def steps_of(stream_key, shape, pieces, least, largest):
    def one(position, blocks):
        steps = jax.random.uniform(jax.random.fold_in(jax.random.fold_in(stream_key, 6), position), (blocks,), jnp.float32, least / len(pieces), largest / len(pieces))
        return jnp.repeat(jnp.exp(steps), shape[position] // blocks).reshape((-1,) + (1,) * (len(shape) - position - 1))

    loudness = one(*pieces[0])
    for cut in pieces[1:]:
        loudness = loudness * one(*cut)
    return loudness


def normal_values(rng, extent, width, most, cuts=(), held_as=jnp.bfloat16):
    loudness = steps_of(rng, extent, cuts, -0.22, 0.18) if cuts else 1.0
    drawn = jax.random.normal(rng, extent, jnp.float32) * width * loudness
    return jnp.minimum(jnp.maximum(drawn, -most), most).astype(held_as)


def setup_inputs(seed: int = 0) -> dict:
    key_list = jax.random.split(jax.random.key(seed), 9)
    wind_u = normal_values(key_list[0], (LEV, NLAT, NLON), 1.0, 6.0, ((1, 8), (2, 4)), jnp.float32)
    wind_v = normal_values(key_list[1], (LEV, NLAT, NLON), 1.0, 6.0, ((1, 8), (2, 4)), jnp.float32)
    turbines = set_ends(jax.random.randint(key_list[2], (NLAT, NLON), 0, 7), jax.random.fold_in(key_list[2], 1), 0, 6).astype(jnp.int32)
    rotor_level = set_ends(jax.random.randint(key_list[3], (NLAT, NLON), 0, LEV - ROTOR + 1), jax.random.fold_in(key_list[3], 1), 0, LEV - ROTOR).astype(jnp.int32)
    block_source = draw_block_source(jax.random.fold_in(key_list[8], 71), 0)
    block_weight = jnp.clip(jax.random.uniform(key_list[5], (BLOCKS, SLOTS, AY, AY), jnp.float32, 0.0052083335, 0.041666668), 0.0052083335, 0.041666668)
    spectra = jnp.clip(jnp.exp(math.log(1.0) - 4.6051702 * jax.random.uniform(key_list[6], (FREQS, DIRS, NLON, NLAT), jnp.float32) ** steps_of(key_list[6], (FREQS, DIRS, NLON, NLAT), ((2, 32),), -0.2, 0.2)), 0.01, 1.0)
    sea_mask = set_ends((jax.random.randint(key_list[7], (NLON, NLAT), 0, 5) < 4).astype(jnp.int32), jax.random.fold_in(key_list[7], 1), 0, 1)
    return {"wind_u": wind_u, "wind_v": wind_v, "turbines": turbines, "rotor_level": rotor_level, "block_source": block_source, "block_weight": block_weight, "spectra": spectra, "sea_mask": sea_mask}


def laplace(field):
    padded = jnp.pad(field, ((0, 0), (1, 1), (1, 1)))
    beside_all = padded[:, 2:, 1:-1] + padded[:, :-2, 1:-1] + padded[:, 1:-1, 2:] + padded[:, 1:-1, :-2]
    return beside_all - 4.0 * field

def reference(wind_u, wind_v, turbines, rotor_level, block_source, block_weight, spectra, sea_mask):
    wind_speed = jnp.sqrt(wind_u * wind_u + wind_v * wind_v + 0.25)
    levels = jnp.arange(LEV, dtype=jnp.int32)[:, None, None]
    lowest = rotor_level[None, :, :]
    inside = jnp.where((levels >= lowest) & (levels < lowest + ROTOR), 1.0, 0.0).astype(jnp.float32)
    drag_rate = 0.08 * turbines.astype(jnp.float32)[None, :, :] * inside * wind_speed
    wind_u_next = (wind_u + 0.2 * laplace(wind_u)) / (1.0 + drag_rate)
    wind_v_next = (wind_v + 0.2 * laplace(wind_v)) / (1.0 + drag_rate)
    low_u = wind_u_next[0]
    low_v = wind_v_next[0]
    surface = jnp.sqrt(low_u * low_u + low_v * low_v + 0.25)
    stress = jnp.stack([surface * low_u, surface * low_v])
    blocks = stress.reshape(2, BLOCKS, AY, NLON)
    picked = blocks[:, block_source]
    regrid = jnp.einsum('bksr,cbksx->cbrx', block_weight, picked, precision=lax.Precision.HIGHEST)
    wave_stress = jnp.transpose(regrid.reshape(2, NLAT, NLON), (0, 2, 1))
    theta = -jnp.pi / 2 + (jnp.arange(DIRS, dtype=jnp.float32) + 0.5) * (2.0 * jnp.pi / DIRS)
    courant = 0.7 * jnp.power(0.93, jnp.arange(FREQS, dtype=jnp.float32))
    cos_dir = jnp.cos(theta)[None, :, None, None]
    sin_dir = jnp.sin(theta)[None, :, None, None]
    speed_f = courant[:, None, None, None]
    cx = speed_f * cos_dir
    cy = speed_f * sin_dir
    padded = jnp.pad(spectra, ((0, 0), (0, 0), (1, 1), (1, 1)))
    west_side = padded[:, :, :-2, 1:-1]
    east_side = padded[:, :, 2:, 1:-1]
    south_side = padded[:, :, 1:-1, :-2]
    north_side = padded[:, :, 1:-1, 2:]
    advected = spectra - jnp.maximum(cx, 0.0) * (spectra - west_side)
    advected = advected - jnp.minimum(cx, 0.0) * (east_side - spectra)
    advected = advected - jnp.maximum(cy, 0.0) * (spectra - south_side)
    advected = advected - jnp.minimum(cy, 0.0) * (north_side - spectra)
    energy = lax.optimization_barrier(jnp.sum(advected, axis=(0, 1)))
    push = jnp.maximum(0.0, wave_stress[0][None] * jnp.cos(theta)[:, None, None] + wave_stress[1][None] * jnp.sin(theta)[:, None, None])
    fraction = jnp.arange(FREQS, dtype=jnp.float32) / (FREQS - 1)
    beta = (0.1 + 0.4 * fraction)[:, None, None, None]
    dissip = (0.05 + 0.5 * fraction)[:, None, None, None]
    growth = 1.0 + beta * push[None]
    damping = 1.0 + dissip * energy[None, None] / (0.2 * FREQS * DIRS)
    spectra_next = sea_mask.astype(jnp.float32)[None, None] * advected * growth / damping
    return (wind_u_next, wind_v_next, spectra_next)
```

```python
import functools
import math

import jax
import jax.numpy as jnp
from jax import lax
from jax.experimental import pallas as pl
from jax.experimental.pallas import tpu as pltpu
from jax.sharding import PartitionSpec as P

ROTOR = 3
LOADS = 6
HALO_CUTS = 4
TILE = 8
MESH = pl.DeviceIdType.MESH
F32 = jnp.float32


def angles(dirs):
    out = []
    for d in range(dirs):
        theta = -math.pi / 2 + (d + 0.5) * (2.0 * math.pi / dirs)
        out.append((math.cos(theta), math.sin(theta)))
    return out


def direction_split(dirs):
    west = [c > 0 for c, _ in angles(dirs)]
    split = sum(west)
    assert all(west[:split]) and not any(west[split:])
    return split


def iota(shape, axis):
    return lax.broadcasted_iota(jnp.int32, shape, axis)


def exchange_kernel(
    sizes,
    u_hbm, v_hbm, turb_hbm, rotor_hbm, source_hbm, weight_hbm, mask_hbm, spectra_hbm,
    out_ref, u_out, v_out,
    x_ref, edge_to_w, edge_to_e, halo_w, halo_e, u_ref, v_ref, turb_ref, rotor_ref, weight_ref, mask_ref, source_ref,
    col_send, col_recv, row_recv, pack_ref, lat_recv, side_send, side_recv, sum_send, sum_recv,
    mix_ref, lat_ref, push_ref, push_w, push_e, scale_w, scale_e,
    load_sem, x_sem, halo_send_sem, halo_recv_sem, col_send_sem, col_recv_sem, row_send_sem, row_recv_sem,
    lat_send_sem, lat_recv_sem, side_send_sem, side_recv_sem, sum_send_sem, sum_recv_sem,
):
    gx_n, gy_n = sizes
    freqs, dirs, lons, lats = x_ref.shape
    levels, rows, width = u_ref.shape
    split = direction_split(dirs)
    gx, gy = lax.axis_index("gx"), lax.axis_index("gy")
    tile = gx * gy_n + gy
    tiles = gx_n * gy_n
    east = tile + 1
    west = tile - 1
    east_id = (lax.rem(east, tiles) // gy_n, lax.rem(east, gy_n))
    west_id = (lax.rem(west + tiles, tiles) // gy_n, lax.rem(west + tiles, gy_n))
    has_east, has_west = tile < tiles - 1, tile > 0
    has = (gx > 0, gx < gx_n - 1, gy > 0, gy < gy_n - 1)
    side_id = ((gx - 1, gy), (gx + 1, gy), (gx, gy - 1), (gx, gy + 1))
    first, last = gy == 0, gy == gy_n - 1
    assert gy_n > 1 and rows == 2 * TILE and rows * gy_n == lats and lons * gy_n == width

    edges = [
        pltpu.make_async_copy(spectra_hbm.at[:, pl.ds(0, split), lons - 1, :], edge_to_e, load_sem.at[7]),
        pltpu.make_async_copy(spectra_hbm.at[:, pl.ds(split, dirs - split), 0, :], edge_to_w, load_sem.at[8]),
    ]
    local = [
        pltpu.make_async_copy(src, dst, load_sem.at[i])
        for i, (src, dst) in enumerate(
            (
                (u_hbm, u_ref), (v_hbm, v_ref), (turb_hbm, turb_ref), (rotor_hbm, rotor_ref),
                (weight_hbm, weight_ref), (source_hbm, source_ref), (mask_hbm, mask_ref),
            )
        )
    ]
    for copy in local[:4] + edges + local[4:]:
        copy.start()
    per_load = freqs // LOADS

    def load(i):
        part = pl.ds(i * per_load, per_load)
        return pltpu.make_async_copy(spectra_hbm.at[part], x_ref.at[part], x_sem.at[i])

    for i in range(LOADS):
        load(i).start()

    barrier = pltpu.get_barrier_semaphore()

    def greet(who):
        pl.semaphore_signal(barrier, inc=1, device_id=who, device_id_type=MESH)

    for step in range(1, gy_n):
        greet((gx, lax.rem(gy + step, gy_n)))
    for there, edge, at in ((has[0], first, gx - 1), (has[1], last, gx + 1)):

        @pl.when(there)
        def _():
            greet((at, gy))

        @pl.when(there & edge)
        def _():
            for j in range(gy_n):
                greet((at, j))

    expected = gy_n - 1 + 2 * has[0].astype(jnp.int32) + 2 * has[1].astype(jnp.int32)

    local[0].wait()
    local[1].wait()
    local[2].wait()
    local[3].wait()
    lane = iota((rows, width), 1)
    row = iota((rows, width), 0)
    rate = 0.08 * turb_ref[...].astype(F32)
    lowest = rotor_ref[...]

    def drag_of(level):
        own = (u_ref[level], v_ref[level])
        speed = jnp.sqrt(own[0] * own[0] + own[1] * own[1] + 0.25)
        inside = jnp.where((level >= lowest) & (level < lowest + ROTOR), 1.0, 0.0).astype(F32)
        return 1.0 + rate * inside * speed

    half = width // 2
    span = lons + 2
    assert 2 * span + lons <= half
    lane_t = iota((TILE, width), 1)
    in_half = lax.rem(lane_t, half)
    low = [u_ref[0], v_ref[0], drag_of(0)]

    def turned(x, by):
        by = by % width
        return pltpu.roll(x, by, 1) if by else x

    def halves(shifts):
        out = []
        for h in range(2):
            parts = [turned(x[h * TILE : (h + 1) * TILE], h * half + s) for x, s in zip(low, shifts)]
            block = jnp.where(in_half < span, parts[0], parts[1])
            if len(parts) == 3:
                block = jnp.where(in_half < 2 * span, block, parts[2])
            out.append(block)
        return jnp.where(lane_t < half, out[0], out[1])

    for p in range(gy_n):
        pack_ref[p] = halves((1 - p * lons, span + 1 - p * lons, 2 * span - p * lons))
    side_send[0] = halves((span - 1, 2 * span - 1))
    side_send[1] = halves((1 - width, span + 1 - width))
    lat_recv[gy] = pack_ref[gy]

    for side in range(2):
        at = 0 if side == 0 else width - 1
        packed = jnp.zeros((rows, width), F32)
        for field, ref in enumerate((u_ref, v_ref)):
            for level in range(levels):
                slot = field * levels + level
                packed = jnp.where(lane == slot, pltpu.roll(ref[level], (slot - at) % width, 1), packed)
        col_send[side] = packed

    def turn(count, begin):
        theta = -math.pi / 2 + (iota((count, lats), 0).astype(F32) + (begin + 0.5)) * (2.0 * math.pi / dirs)
        return jnp.abs(jnp.cos(theta))

    turn_w, turn_e = turn(split, 0), turn(dirs - split, split)
    for copy in edges:
        copy.wait()

    def add_edges(f, carry):
        to_e, to_w, courant = carry
        return to_e + courant * edge_to_e[f], to_w + courant * edge_to_w[f], courant * 0.93

    sums = lax.fori_loop(
        0, freqs, add_edges,
        (jnp.zeros((split, lats), F32), jnp.zeros((dirs - split, lats), F32), jnp.float32(0.7)), unroll=4,
    )
    sum_send[0] = jnp.sum(turn_e * sums[1], axis=0, keepdims=True)
    sum_send[1] = jnp.sum(turn_w * sums[0], axis=0, keepdims=True)

    pl.semaphore_wait(barrier, expected)

    def sum_copy(to_east):
        return pltpu.make_async_remote_copy(
            src_ref=sum_send.at[int(to_east)],
            dst_ref=sum_recv.at[int(to_east)],
            send_sem=sum_send_sem.at[int(to_east)],
            recv_sem=sum_recv_sem.at[int(to_east)],
            device_id=east_id if to_east else west_id,
            device_id_type=MESH,
        )

    def side_copy(to_east):
        return pltpu.make_async_remote_copy(
            src_ref=side_send.at[int(to_east)],
            dst_ref=side_recv.at[gy],
            send_sem=side_send_sem.at[int(to_east)],
            recv_sem=side_recv_sem.at[gy],
            device_id=(gx + 1, 0) if to_east else (gx - 1, gy_n - 1),
            device_id_type=MESH,
        )

    def side_arrival(j):
        return pltpu.make_async_remote_copy(
            src_ref=side_send.at[0],
            dst_ref=side_recv.at[j],
            send_sem=side_send_sem.at[0],
            recv_sem=side_recv_sem.at[j],
            device_id=east_id,
            device_id_type=MESH,
        )

    def lat_copy(step):
        return pltpu.make_async_remote_copy(
            src_ref=pack_ref.at[lax.rem(gy + step, gy_n)],
            dst_ref=lat_recv.at[gy],
            send_sem=lat_send_sem.at[step - 1],
            recv_sem=lat_recv_sem.at[step - 1],
            device_id=(gx, lax.rem(gy + step, gy_n)),
            device_id_type=MESH,
        )

    def lat_arrival(step):
        return pltpu.make_async_remote_copy(
            src_ref=pack_ref.at[gy],
            dst_ref=lat_recv.at[lax.rem(gy - step + gy_n, gy_n)],
            send_sem=lat_send_sem.at[step - 1],
            recv_sem=lat_recv_sem.at[step - 1],
            device_id=(gx, lax.rem(gy + step, gy_n)),
            device_id_type=MESH,
        )

    def row_copy(field, to_upper):
        ref = (u_ref, v_ref)[field]
        slot = 0 if to_upper else 1
        return pltpu.make_async_remote_copy(
            src_ref=ref.at[:, rows - 1 if to_upper else 0, :],
            dst_ref=row_recv.at[slot, field],
            send_sem=row_send_sem.at[slot, field],
            recv_sem=row_recv_sem.at[slot, field],
            device_id=side_id[3 if to_upper else 2],
            device_id_type=MESH,
        )

    def col_copy(side):
        return pltpu.make_async_remote_copy(
            src_ref=col_send.at[side],
            dst_ref=col_recv.at[1 - side],
            send_sem=col_send_sem.at[side],
            recv_sem=col_recv_sem.at[1 - side],
            device_id=side_id[side],
            device_id_type=MESH,
        )

    per_cut = freqs // HALO_CUTS

    def halo_copy(to_east, i):
        part = pl.ds(i * per_cut, per_cut)
        return pltpu.make_async_remote_copy(
            src_ref=(edge_to_e if to_east else edge_to_w).at[part],
            dst_ref=(halo_w if to_east else halo_e).at[part],
            send_sem=halo_send_sem.at[int(to_east), i],
            recv_sem=halo_recv_sem.at[int(to_east), i],
            device_id=east_id if to_east else west_id,
            device_id_type=MESH,
        )

    neighbours = ((True, has_east), (False, has_west))
    arrivals = ((True, has_west), (False, has_east))
    beyond = ((True, has[1]), (False, has[0]))

    for to_east, there in beyond:

        @pl.when(there)
        def _():
            side_copy(to_east).start()

    for to_east, there in neighbours:

        @pl.when(there)
        def _():
            sum_copy(to_east).start()

    for step in range(1, gy_n):
        lat_copy(step).start()

    for to_upper in (False, True):

        @pl.when(has[3 if to_upper else 2])
        def _():
            for field in range(2):
                row_copy(field, to_upper).start()

    for side in range(2):

        @pl.when(has[side])
        def _():
            col_copy(side).start()

    for i in range(HALO_CUTS):
        for to_east, there in neighbours:

            @pl.when(there)
            def _():
                halo_copy(to_east, i).start()

    for to_east, there in arrivals:

        @pl.when(jnp.logical_not(there))
        def _():
            halo = halo_w if to_east else halo_e
            halo[...] = jnp.zeros_like(halo)
            sum_recv[int(to_east)] = jnp.zeros((1, lats), F32)

    for edge, there in ((first, has[0]), (last, has[1])):

        @pl.when(edge & jnp.logical_not(there))
        def _():
            side_recv[...] = jnp.zeros_like(side_recv)

    row_in = iota((lons, lats), 0)
    lane_in = iota((lons, lats), 1)
    keep_w = jnp.where(row_in == 0, 0.0, 1.0).astype(F32)
    keep_e = jnp.where(row_in == lons - 1, 0.0, 1.0).astype(F32)
    keep_s = jnp.where(lane_in == 0, 0.0, 1.0).astype(F32)
    keep_n = jnp.where(lane_in == lats - 1, 0.0, 1.0).astype(F32)
    turns = angles(dirs)

    def advect(f, carry):
        total, courant = carry
        for d, (cos_d, sin_d) in enumerate(turns):
            x = x_ref[f, d]
            a = courant * abs(cos_d)
            b = courant * abs(sin_d)
            if cos_d > 0:
                along = (a * keep_w) * pltpu.roll(x, 1, 0)
            else:
                along = (a * keep_e) * pltpu.roll(x, lons - 1, 0)
            if sin_d > 0:
                across = (b * keep_s) * pltpu.roll(x, 1, 1)
            else:
                across = (b * keep_n) * pltpu.roll(x, lats - 1, 1)
            moved = (1.0 - a - b) * x + along + across
            out_ref[f, d] = moved
            total = total + moved
        return total, courant * 0.93

    carry = (jnp.zeros((lons, lats), F32), jnp.float32(0.7))
    for i in range(LOADS):
        load(i).wait()
        carry = lax.fori_loop(i * per_load, (i + 1) * per_load, advect, carry)
    total = carry[0]

    local[4].wait()
    local[5].wait()
    local[6].wait()
    blocks, slots = weight_ref.shape[0], weight_ref.shape[1]
    block_of = iota((rows, lats), 1) // rows
    wide, picks = [], []
    for k in range(slots):
        wide.append(jnp.concatenate([weight_ref[b, k] for b in range(blocks)], axis=1))
        pick = jnp.zeros((rows, lats), jnp.int32)
        for b in range(blocks):
            pick = jnp.where(block_of == b, source_ref[k, b], pick)
        picks.append(pick)
    for source in range(blocks):
        part = jnp.zeros((rows, lats), F32)
        for k in range(slots):
            part = part + jnp.where(picks[k] == source, wide[k], 0.0)
        mix_ref[source * rows : (source + 1) * rows, :] = part

    for step in range(1, gy_n):
        lat_arrival(step).wait_recv()
    for edge, there in ((first, has[0]), (last, has[1])):

        @pl.when(edge & there)
        def _():
            for j in range(gy_n):
                side_arrival(j).wait_recv()

    beside = jnp.where(first, 0, jnp.where(last, span - 1, -width))
    from_side = (in_half == beside) | (in_half == beside + span)
    for j in range(gy_n):
        block = jnp.where(from_side, side_recv[j], lat_recv[j])
        lat_ref[j * rows : j * rows + TILE, :] = block
        lat_ref[j * rows + TILE : (j + 1) * rows, :] = pltpu.roll(block, half, 1)
    low_all = lat_ref[...]
    lat_row = iota((lats, width), 0)
    lat_lane = iota((lats, width), 1)
    lower = jnp.where(lat_row == 0, 0.0, pltpu.roll(low_all, 1, 0))
    upper = jnp.where(lat_row == lats - 1, 0.0, pltpu.roll(low_all, lats - 1, 0))
    around = upper + lower + pltpu.roll(low_all, width - 1, 1) + pltpu.roll(low_all, 1, 1) - 4.0 * low_all
    drag_u, drag_v = turned(low_all, 1 - 2 * span), turned(low_all, 1 - span)
    is_u = (lat_lane >= 1) & (lat_lane <= lons)
    is_v = (lat_lane >= span + 1) & (lat_lane <= span + lons)
    low_next = (low_all + 0.2 * around) / jnp.where(is_u, drag_u, jnp.where(is_v, drag_v, 1.0))
    low_v = turned(low_next, -span)
    surface = jnp.sqrt(low_next * low_next + low_v * low_v + 0.25)
    stress = jnp.where(
        lat_lane < lons, turned(surface * low_next, -1),
        jnp.where(lat_lane < 2 * lons, turned(surface * low_v, lons - 1), 0.0),
    )
    wave = lax.dot_general(
        stress, mix_ref[...], (((0,), (0,)), ((), ())),
        precision=lax.Precision.HIGHEST, preferred_element_type=F32,
    )
    wave_x, wave_y = wave[0:lons], wave[lons : 2 * lons]
    for d, (cos_d, sin_d) in enumerate(turns):
        push = jnp.maximum(0.0, wave_x * cos_d + wave_y * sin_d)
        push_ref[d] = push
        if d < split:
            push_w[d : d + 1, :] = push[0:1]
        else:
            push_e[d - split : d - split + 1, :] = push[lons - 1 : lons]

    for to_east, there in arrivals:

        @pl.when(there)
        def _():
            sum_copy(to_east).wait_recv()

    energy = total + jnp.where(row_in == 0, sum_recv[1], 0.0) + jnp.where(row_in == lons - 1, sum_recv[0], 0.0)
    energy = energy / (0.2 * freqs * dirs)
    mask = mask_ref[...].astype(F32)

    def settle(f, carry):
        fraction = f.astype(F32) / (freqs - 1)
        scale = mask / (1.0 + (0.05 + 0.5 * fraction) * energy)
        grow = scale * (0.1 + 0.4 * fraction)
        scale_w[f] = scale[0:1]
        scale_e[f] = scale[lons - 1 : lons]
        for d in range(dirs):
            out_ref[f, d] = out_ref[f, d] * (scale + grow * push_ref[d])
        return carry

    lax.fori_loop(0, freqs, settle, 0)

    for side in range(2):

        @pl.when(has[side])
        def _():
            col_copy(1 - side).wait_recv()

        @pl.when(jnp.logical_not(has[side]))
        def _():
            col_recv[side] = jnp.zeros((rows, width), F32)

        @pl.when(has[2 + side])
        def _():
            for field in range(2):
                row_copy(field, side == 0).wait_recv()

        @pl.when(jnp.logical_not(has[2 + side]))
        def _():
            row_recv[side] = jnp.zeros_like(row_recv[side])

    for level in range(levels):
        drag = drag_of(level)
        for field, (ref, out) in enumerate(((u_ref, u_out), (v_ref, v_out))):
            x = ref[level]
            slot = field * levels + level
            down = jnp.where(row == 0, row_recv[0, field, level : level + 1, :], pltpu.roll(x, 1, 0))
            up = jnp.where(row == rows - 1, row_recv[1, field, level : level + 1, :], pltpu.roll(x, rows - 1, 0))
            left = jnp.where(lane == 0, pltpu.roll(col_recv[0], (0 - slot) % width, 1), pltpu.roll(x, 1, 1))
            right = jnp.where(
                lane == width - 1, pltpu.roll(col_recv[1], (width - 1 - slot) % width, 1), pltpu.roll(x, width - 1, 1)
            )
            out[level] = (x + 0.2 * (up + down + right + left - 4.0 * x)) / drag

    top, bottom = pl.ds(0, TILE), pl.ds(lons - TILE, TILE)
    row_t = iota((TILE, lats), 0)

    def mend(f, courant):
        beta = 0.1 + 0.4 * (f.astype(F32) / (freqs - 1))
        halo_w[f] = (courant * turn_w) * halo_w[f] * (scale_w[f] * (1.0 + beta * push_w[...]))
        halo_e[f] = (courant * turn_e) * halo_e[f] * (scale_e[f] * (1.0 + beta * push_e[...]))
        for d in range(split):
            out_ref[f, d, top, :] += jnp.where(row_t == 0, halo_w[f, d : d + 1, :], 0.0)
        for d in range(split, dirs):
            out_ref[f, d, bottom, :] += jnp.where(row_t == TILE - 1, halo_e[f, d - split : d - split + 1, :], 0.0)
        return courant * 0.93

    courant = jnp.float32(0.7)
    for i in range(HALO_CUTS):
        for to_east, there in arrivals:

            @pl.when(there)
            def _():
                halo_copy(to_east, i).wait_recv()

        courant = lax.fori_loop(i * per_cut, (i + 1) * per_cut, mend, courant)

    for to_east, there in beyond:

        @pl.when(there)
        def _():
            side_copy(to_east).wait_send()

    for to_east, there in neighbours:

        @pl.when(there)
        def _():
            sum_copy(to_east).wait_send()
            for i in range(HALO_CUTS):
                halo_copy(to_east, i).wait_send()

    for step in range(1, gy_n):
        lat_copy(step).wait_send()

    for to_upper in (False, True):

        @pl.when(has[3 if to_upper else 2])
        def _():
            for field in range(2):
                row_copy(field, to_upper).wait_send()

    for side in range(2):

        @pl.when(has[side])
        def _():
            col_copy(side).wait_send()


def write_kernel(done_ref, u_ref, v_ref, out_hbm, u_hbm, v_hbm, out_sem, wind_sem):
    freqs = done_ref.shape[0]
    winds = [
        pltpu.make_async_copy(u_ref, u_hbm, wind_sem.at[0]),
        pltpu.make_async_copy(v_ref, v_hbm, wind_sem.at[1]),
    ]
    parts = [pltpu.make_async_copy(done_ref.at[f], out_hbm.at[f], out_sem.at[f]) for f in range(freqs)]
    for copy in winds + parts:
        copy.start()
    for copy in winds + parts:
        copy.wait()


def solution(mesh):
    gx_n, gy_n = mesh.shape["gx"], mesh.shape["gy"]
    vmem = pl.BlockSpec(memory_space=pltpu.VMEM)
    anywhere = pl.BlockSpec(memory_space=pltpu.HBM)

    def per_device(wind_u, wind_v, turbines, rotor_level, block_source, block_weight, spectra, sea_mask):
        freqs, dirs, lons, lats = spectra.shape
        levels, rows, width = wind_u.shape
        split = direction_split(dirs)
        dma = pltpu.SemaphoreType.DMA

        def in_hbm(x):
            return pltpu.with_memory_space_constraint(x, pltpu.HBM)

        done, u_next, v_next = pl.pallas_call(
            functools.partial(exchange_kernel, (gx_n, gy_n)),
            out_shape=(
                pltpu.VMEM(spectra.shape, F32),
                pltpu.VMEM(wind_u.shape, F32),
                pltpu.VMEM(wind_u.shape, F32),
            ),
            in_specs=[anywhere] * 8,
            out_specs=(vmem,) * 3,
            scratch_shapes=[
                pltpu.VMEM(spectra.shape, F32),
                pltpu.VMEM((freqs, dirs - split, lats), F32),
                pltpu.VMEM((freqs, split, lats), F32),
                pltpu.VMEM((freqs, split, lats), F32),
                pltpu.VMEM((freqs, dirs - split, lats), F32),
                pltpu.VMEM(wind_u.shape, F32),
                pltpu.VMEM(wind_u.shape, F32),
                pltpu.VMEM((rows, width), jnp.int32),
                pltpu.VMEM((rows, width), jnp.int32),
                pltpu.VMEM(block_weight.shape, F32),
                pltpu.VMEM((lons, lats), jnp.int32),
                pltpu.SMEM(block_source.shape[::-1], jnp.int32),
                pltpu.VMEM((2, rows, width), F32),
                pltpu.VMEM((2, rows, width), F32),
                pltpu.VMEM((2, 2, levels, width), F32),
                pltpu.VMEM((gy_n, TILE, width), F32),
                pltpu.VMEM((gy_n, TILE, width), F32),
                pltpu.VMEM((2, TILE, width), F32),
                pltpu.VMEM((gy_n, TILE, width), F32),
                pltpu.VMEM((2, 1, lats), F32),
                pltpu.VMEM((2, 1, lats), F32),
                pltpu.VMEM((lats, lats), F32),
                pltpu.VMEM((lats, width), F32),
                pltpu.VMEM((dirs, lons, lats), F32),
                pltpu.VMEM((split, lats), F32),
                pltpu.VMEM((dirs - split, lats), F32),
                pltpu.VMEM((freqs, 1, lats), F32),
                pltpu.VMEM((freqs, 1, lats), F32),
                dma((9,)),
                dma((LOADS,)),
                dma((2, HALO_CUTS)),
                dma((2, HALO_CUTS)),
                dma((2,)),
                dma((2,)),
                dma((2, 2)),
                dma((2, 2)),
                dma((gy_n - 1,)),
                dma((gy_n - 1,)),
                dma((2,)),
                dma((gy_n,)),
                dma((2,)),
                dma((2,)),
            ],
            compiler_params=pltpu.CompilerParams(
                collective_id=0, has_side_effects=True, vmem_limit_bytes=24 * 2**20
            ),
        )(
            in_hbm(wind_u), in_hbm(wind_v), in_hbm(turbines), in_hbm(rotor_level), in_hbm(block_source.T),
            in_hbm(block_weight), in_hbm(sea_mask), in_hbm(spectra),
        )
        spectra_next, u_done, v_done = pl.pallas_call(
            write_kernel,
            out_shape=(
                jax.ShapeDtypeStruct(spectra.shape, F32),
                jax.ShapeDtypeStruct(wind_u.shape, F32),
                jax.ShapeDtypeStruct(wind_u.shape, F32),
            ),
            in_specs=[vmem] * 3,
            out_specs=(anywhere,) * 3,
            scratch_shapes=[dma((freqs,)), dma((2,))],
            compiler_params=pltpu.CompilerParams(vmem_limit_bytes=2 * 2**20),
        )(done, u_next, v_next)
        return u_done, v_done, spectra_next

    in_specs = (
        P(None, "gy", "gx"),
        P(None, "gy", "gx"),
        P("gy", "gx"),
        P("gy", "gx"),
        P(),
        P(),
        P(None, None, ("gx", "gy"), None),
        P(("gx", "gy"), None),
    )
    out_specs = (P(None, "gy", "gx"), P(None, "gy", "gx"), P(None, None, ("gx", "gy"), None))
    return jax.shard_map(per_device, mesh=mesh, in_specs=in_specs, out_specs=out_specs, check_vma=False)
```

```python
import functools
import math

import jax
import jax.numpy as jnp
from jax import lax
from jax.experimental import pallas as pl
from jax.experimental.pallas import tpu as pltpu
from jax.sharding import PartitionSpec as P

ROTOR = 3
LOADS = 6
HALO_CUTS = 4
HOLD_Z = 3
HOLD_D = 2
TILE = 8
MESH = pl.DeviceIdType.MESH
F32 = jnp.float32


def angles(dirs):
    out = []
    for d in range(dirs):
        theta = -math.pi / 2 + (d + 0.5) * (2.0 * math.pi / dirs)
        out.append((math.cos(theta), math.sin(theta)))
    return out


def direction_split(dirs):
    west = [c > 0 for c, _ in angles(dirs)]
    split = sum(west)
    assert all(west[:split]) and not any(west[split:])
    return split


def iota(shape, axis):
    return lax.broadcasted_iota(jnp.int32, shape, axis)


def exchange_kernel(
    sizes,
    u_hbm, v_hbm, turb_hbm, rotor_hbm, source_hbm, weight_hbm, spectra_hbm,
    adv_ref, edge_w_ref, edge_e_ref, energy_ref, push_ref, u_out, v_out,
    x_ref, edge_to_w, edge_to_e, halo_w, halo_e, u_ref, v_ref, turb_ref, rotor_ref, weight_ref, source_ref,
    col_send, col_recv, row_recv, pack_ref, lat_recv, side_send, side_recv, mix_ref, lat_ref,
    load_sem, x_sem, halo_send_sem, halo_recv_sem, col_send_sem, col_recv_sem, row_send_sem, row_recv_sem,
    lat_send_sem, lat_recv_sem, side_send_sem, side_recv_sem,
):
    gx_n, gy_n = sizes
    freqs, dirs, lons, lats = x_ref.shape
    levels, rows, width = u_ref.shape
    split = direction_split(dirs)
    gx, gy = lax.axis_index("gx"), lax.axis_index("gy")
    tile = gx * gy_n + gy
    tiles = gx_n * gy_n
    east = tile + 1
    west = tile - 1
    east_id = (lax.rem(east, tiles) // gy_n, lax.rem(east, gy_n))
    west_id = (lax.rem(west + tiles, tiles) // gy_n, lax.rem(west + tiles, gy_n))
    has_east, has_west = tile < tiles - 1, tile > 0
    has = (gx > 0, gx < gx_n - 1, gy > 0, gy < gy_n - 1)
    side_id = ((gx - 1, gy), (gx + 1, gy), (gx, gy - 1), (gx, gy + 1))
    first, last = gy == 0, gy == gy_n - 1
    assert gy_n > 1 and rows == 2 * TILE and rows * gy_n == lats and lons * gy_n == width

    edge_loads = [
        pltpu.make_async_copy(spectra_hbm.at[:, pl.ds(0, split), lons - 1, :], edge_to_e, load_sem.at[6]),
        pltpu.make_async_copy(spectra_hbm.at[:, pl.ds(split, dirs - split), 0, :], edge_to_w, load_sem.at[7]),
    ]
    local = [
        pltpu.make_async_copy(src, dst, load_sem.at[i])
        for i, (src, dst) in enumerate(
            (
                (u_hbm, u_ref), (v_hbm, v_ref), (turb_hbm, turb_ref), (rotor_hbm, rotor_ref),
                (weight_hbm, weight_ref), (source_hbm, source_ref),
            )
        )
    ]
    for copy in local[:4] + edge_loads + local[4:]:
        copy.start()
    per_load = freqs // LOADS

    def load(i):
        part = pl.ds(i * per_load, per_load)
        return pltpu.make_async_copy(spectra_hbm.at[part], x_ref.at[part], x_sem.at[i])

    for i in range(LOADS):
        load(i).start()

    barrier = pltpu.get_barrier_semaphore()

    def greet(who):
        pl.semaphore_signal(barrier, inc=1, device_id=who, device_id_type=MESH)

    for step in range(1, gy_n):
        greet((gx, lax.rem(gy + step, gy_n)))
    for there, edge, at in ((has[0], first, gx - 1), (has[1], last, gx + 1)):

        @pl.when(there)
        def _():
            greet((at, gy))

        @pl.when(there & edge)
        def _():
            for j in range(gy_n):
                greet((at, j))

    expected = gy_n - 1 + 2 * has[0].astype(jnp.int32) + 2 * has[1].astype(jnp.int32)

    local[0].wait()
    local[1].wait()
    local[2].wait()
    local[3].wait()
    lane = iota((rows, width), 1)
    row = iota((rows, width), 0)
    rate = 0.08 * turb_ref[...].astype(F32)
    lowest = rotor_ref[...]

    def drag_of(level):
        own = (u_ref[level], v_ref[level])
        speed = jnp.sqrt(own[0] * own[0] + own[1] * own[1] + 0.25)
        inside = jnp.where((level >= lowest) & (level < lowest + ROTOR), 1.0, 0.0).astype(F32)
        return 1.0 + rate * inside * speed

    half = width // 2
    span = lons + 2
    assert 2 * span + lons <= half
    lane_t = iota((TILE, width), 1)
    in_half = lax.rem(lane_t, half)
    low = [u_ref[0], v_ref[0], drag_of(0)]

    def turned(x, by):
        by = by % width
        return pltpu.roll(x, by, 1) if by else x

    def halves(shifts):
        out = []
        for h in range(2):
            parts = [turned(x[h * TILE : (h + 1) * TILE], h * half + s) for x, s in zip(low, shifts)]
            block = jnp.where(in_half < span, parts[0], parts[1])
            if len(parts) == 3:
                block = jnp.where(in_half < 2 * span, block, parts[2])
            out.append(block)
        return jnp.where(lane_t < half, out[0], out[1])

    for p in range(gy_n):
        pack_ref[p] = halves((1 - p * lons, span + 1 - p * lons, 2 * span - p * lons))
    side_send[0] = halves((span - 1, 2 * span - 1))
    side_send[1] = halves((1 - width, span + 1 - width))
    lat_recv[gy] = pack_ref[gy]

    for side in range(2):
        at = 0 if side == 0 else width - 1
        packed = jnp.zeros((rows, width), F32)
        for field, ref in enumerate((u_ref, v_ref)):
            for level in range(levels):
                slot = field * levels + level
                packed = jnp.where(lane == slot, pltpu.roll(ref[level], (slot - at) % width, 1), packed)
        col_send[side] = packed

    pl.semaphore_wait(barrier, expected)

    def side_copy(to_east):
        return pltpu.make_async_remote_copy(
            src_ref=side_send.at[int(to_east)],
            dst_ref=side_recv.at[gy],
            send_sem=side_send_sem.at[int(to_east)],
            recv_sem=side_recv_sem.at[gy],
            device_id=(gx + 1, 0) if to_east else (gx - 1, gy_n - 1),
            device_id_type=MESH,
        )

    def side_arrival(j):
        return pltpu.make_async_remote_copy(
            src_ref=side_send.at[0],
            dst_ref=side_recv.at[j],
            send_sem=side_send_sem.at[0],
            recv_sem=side_recv_sem.at[j],
            device_id=east_id,
            device_id_type=MESH,
        )

    def lat_copy(step):
        return pltpu.make_async_remote_copy(
            src_ref=pack_ref.at[lax.rem(gy + step, gy_n)],
            dst_ref=lat_recv.at[gy],
            send_sem=lat_send_sem.at[step - 1],
            recv_sem=lat_recv_sem.at[step - 1],
            device_id=(gx, lax.rem(gy + step, gy_n)),
            device_id_type=MESH,
        )

    def lat_arrival(step):
        return pltpu.make_async_remote_copy(
            src_ref=pack_ref.at[gy],
            dst_ref=lat_recv.at[lax.rem(gy - step + gy_n, gy_n)],
            send_sem=lat_send_sem.at[step - 1],
            recv_sem=lat_recv_sem.at[step - 1],
            device_id=(gx, lax.rem(gy + step, gy_n)),
            device_id_type=MESH,
        )

    def row_copy(field, to_upper):
        ref = (u_ref, v_ref)[field]
        slot = 0 if to_upper else 1
        return pltpu.make_async_remote_copy(
            src_ref=ref.at[:, rows - 1 if to_upper else 0, :],
            dst_ref=row_recv.at[slot, field],
            send_sem=row_send_sem.at[slot, field],
            recv_sem=row_recv_sem.at[slot, field],
            device_id=side_id[3 if to_upper else 2],
            device_id_type=MESH,
        )

    def col_copy(side):
        return pltpu.make_async_remote_copy(
            src_ref=col_send.at[side],
            dst_ref=col_recv.at[1 - side],
            send_sem=col_send_sem.at[side],
            recv_sem=col_recv_sem.at[1 - side],
            device_id=side_id[side],
            device_id_type=MESH,
        )

    per_cut = freqs // HALO_CUTS

    def halo_copy(to_east, i):
        part = pl.ds(i * per_cut, per_cut)
        return pltpu.make_async_remote_copy(
            src_ref=(edge_to_e if to_east else edge_to_w).at[part],
            dst_ref=(halo_w if to_east else halo_e).at[part],
            send_sem=halo_send_sem.at[int(to_east), i],
            recv_sem=halo_recv_sem.at[int(to_east), i],
            device_id=east_id if to_east else west_id,
            device_id_type=MESH,
        )

    neighbours = ((True, has_east), (False, has_west))
    arrivals = ((True, has_west), (False, has_east))
    beyond = ((True, has[1]), (False, has[0]))

    for to_east, there in beyond:

        @pl.when(there)
        def _():
            side_copy(to_east).start()

    for step in range(1, gy_n):
        lat_copy(step).start()

    for to_upper in (False, True):

        @pl.when(has[3 if to_upper else 2])
        def _():
            for field in range(2):
                row_copy(field, to_upper).start()

    for side in range(2):

        @pl.when(has[side])
        def _():
            col_copy(side).start()

    for copy in edge_loads:
        copy.wait()
    far_east, far_west = lax.rem(gy, 4) == 3, lax.rem(gy, 4) == 0
    held = {}
    for to_east, there in neighbours:
        far = far_east if to_east else far_west
        over = last if to_east else first
        held.setdefault(0, []).append((to_east, there & jnp.logical_not(far)))
        held.setdefault(HOLD_D, []).append((to_east, there & far & jnp.logical_not(over)))
        held.setdefault(HOLD_Z, []).append((to_east, there & far & over))

    def send_halos(stage):
        for to_east, there in held.get(stage, []):

            @pl.when(there)
            def _():
                for i in range(HALO_CUTS):
                    halo_copy(to_east, i).start()

    send_halos(0)

    for to_east, there in arrivals:

        @pl.when(jnp.logical_not(there))
        def _():
            halo = halo_w if to_east else halo_e
            halo[...] = jnp.zeros_like(halo)

    for edge, there in ((first, has[0]), (last, has[1])):

        @pl.when(edge & jnp.logical_not(there))
        def _():
            side_recv[...] = jnp.zeros_like(side_recv)

    row_in = iota((lons, lats), 0)
    lane_in = iota((lons, lats), 1)
    keep_w = jnp.where(row_in == 0, 0.0, 1.0).astype(F32)
    keep_e = jnp.where(row_in == lons - 1, 0.0, 1.0).astype(F32)
    keep_s = jnp.where(lane_in == 0, 0.0, 1.0).astype(F32)
    keep_n = jnp.where(lane_in == lats - 1, 0.0, 1.0).astype(F32)
    turns = angles(dirs)

    def advect(f, carry):
        total, courant = carry
        for d, (cos_d, sin_d) in enumerate(turns):
            x = x_ref[f, d]
            a = courant * abs(cos_d)
            b = courant * abs(sin_d)
            if cos_d > 0:
                along = (a * keep_w) * pltpu.roll(x, 1, 0)
            else:
                along = (a * keep_e) * pltpu.roll(x, lons - 1, 0)
            if sin_d > 0:
                across = (b * keep_s) * pltpu.roll(x, 1, 1)
            else:
                across = (b * keep_n) * pltpu.roll(x, lats - 1, 1)
            moved = (1.0 - a - b) * x + along + across
            adv_ref[f, d] = moved
            total = total + moved
        return total, courant * 0.93

    carry = (jnp.zeros((lons, lats), F32), jnp.float32(0.7))
    for i in range(LOADS):
        if i > 0:
            send_halos(i)
        load(i).wait()
        carry = lax.fori_loop(i * per_load, (i + 1) * per_load, advect, carry)
    total = carry[0]

    local[4].wait()
    local[5].wait()
    blocks, slots = weight_ref.shape[0], weight_ref.shape[1]
    block_of = iota((rows, lats), 1) // rows
    wide, picks = [], []
    for k in range(slots):
        wide.append(jnp.concatenate([weight_ref[b, k] for b in range(blocks)], axis=1))
        pick = jnp.zeros((rows, lats), jnp.int32)
        for b in range(blocks):
            pick = jnp.where(block_of == b, source_ref[k, b], pick)
        picks.append(pick)
    for source in range(blocks):
        part = jnp.zeros((rows, lats), F32)
        for k in range(slots):
            part = part + jnp.where(picks[k] == source, wide[k], 0.0)
        mix_ref[source * rows : (source + 1) * rows, :] = part

    for step in range(1, gy_n):
        lat_arrival(step).wait_recv()
    for edge, there in ((first, has[0]), (last, has[1])):

        @pl.when(edge & there)
        def _():
            for j in range(gy_n):
                side_arrival(j).wait_recv()

    beside = jnp.where(first, 0, jnp.where(last, span - 1, -width))
    from_side = (in_half == beside) | (in_half == beside + span)
    for j in range(gy_n):
        block = jnp.where(from_side, side_recv[j], lat_recv[j])
        lat_ref[j * rows : j * rows + TILE, :] = block
        lat_ref[j * rows + TILE : (j + 1) * rows, :] = pltpu.roll(block, half, 1)
    low_all = lat_ref[...]
    lat_row = iota((lats, width), 0)
    lat_lane = iota((lats, width), 1)
    lower = jnp.where(lat_row == 0, 0.0, pltpu.roll(low_all, 1, 0))
    upper = jnp.where(lat_row == lats - 1, 0.0, pltpu.roll(low_all, lats - 1, 0))
    around = upper + lower + pltpu.roll(low_all, width - 1, 1) + pltpu.roll(low_all, 1, 1) - 4.0 * low_all
    drag_u, drag_v = turned(low_all, 1 - 2 * span), turned(low_all, 1 - span)
    is_u = (lat_lane >= 1) & (lat_lane <= lons)
    is_v = (lat_lane >= span + 1) & (lat_lane <= span + lons)
    low_next = (low_all + 0.2 * around) / jnp.where(is_u, drag_u, jnp.where(is_v, drag_v, 1.0))
    low_v = turned(low_next, -span)
    surface = jnp.sqrt(low_next * low_next + low_v * low_v + 0.25)
    stress = jnp.where(
        lat_lane < lons, turned(surface * low_next, -1),
        jnp.where(lat_lane < 2 * lons, turned(surface * low_v, lons - 1), 0.0),
    )
    wave = lax.dot_general(
        stress, mix_ref[...], (((0,), (0,)), ((), ())),
        precision=lax.Precision.HIGHEST, preferred_element_type=F32,
    )
    wave_x, wave_y = wave[0:lons], wave[lons : 2 * lons]
    for d, (cos_d, sin_d) in enumerate(turns):
        push_ref[d] = jnp.maximum(0.0, wave_x * cos_d + wave_y * sin_d)

    for side in range(2):

        @pl.when(has[side])
        def _():
            col_copy(1 - side).wait_recv()

        @pl.when(jnp.logical_not(has[side]))
        def _():
            col_recv[side] = jnp.zeros((rows, width), F32)

        @pl.when(has[2 + side])
        def _():
            for field in range(2):
                row_copy(field, side == 0).wait_recv()

        @pl.when(jnp.logical_not(has[2 + side]))
        def _():
            row_recv[side] = jnp.zeros_like(row_recv[side])

    for level in range(levels):
        drag = drag_of(level)
        for field, (ref, out) in enumerate(((u_ref, u_out), (v_ref, v_out))):
            x = ref[level]
            slot = field * levels + level
            down = jnp.where(row == 0, row_recv[0, field, level : level + 1, :], pltpu.roll(x, 1, 0))
            up = jnp.where(row == rows - 1, row_recv[1, field, level : level + 1, :], pltpu.roll(x, rows - 1, 0))
            left = jnp.where(lane == 0, pltpu.roll(col_recv[0], (0 - slot) % width, 1), pltpu.roll(x, 1, 1))
            right = jnp.where(
                lane == width - 1, pltpu.roll(col_recv[1], (width - 1 - slot) % width, 1), pltpu.roll(x, width - 1, 1)
            )
            out[level] = (x + 0.2 * (up + down + right + left - 4.0 * x)) / drag

    def turn(count, begin):
        theta = -math.pi / 2 + (iota((count, lats), 0).astype(F32) + (begin + 0.5)) * (2.0 * math.pi / dirs)
        return jnp.abs(jnp.cos(theta))

    turn_w, turn_e = turn(split, 0), turn(dirs - split, split)

    def edges(f, carry):
        acc_w, acc_e, courant = carry
        value_w = (courant * turn_w) * halo_w[f]
        value_e = (courant * turn_e) * halo_e[f]
        edge_w_ref[f] = value_w
        edge_e_ref[f] = value_e
        return acc_w + value_w, acc_e + value_e, courant * 0.93

    sums = (jnp.zeros((split, lats), F32), jnp.zeros((dirs - split, lats), F32), jnp.float32(0.7))
    for i in range(HALO_CUTS):
        for to_east, there in arrivals:

            @pl.when(there)
            def _():
                halo_copy(to_east, i).wait_recv()

        sums = lax.fori_loop(i * per_cut, (i + 1) * per_cut, edges, sums)
    sum_w = jnp.sum(sums[0], axis=0, keepdims=True)
    sum_e = jnp.sum(sums[1], axis=0, keepdims=True)
    energy_ref[...] = total + jnp.where(row_in == 0, sum_w, 0.0) + jnp.where(row_in == lons - 1, sum_e, 0.0)

    for to_east, there in beyond:

        @pl.when(there)
        def _():
            side_copy(to_east).wait_send()

    for to_east, there in neighbours:

        @pl.when(there)
        def _():
            for i in range(HALO_CUTS):
                halo_copy(to_east, i).wait_send()

    for step in range(1, gy_n):
        lat_copy(step).wait_send()

    for to_upper in (False, True):

        @pl.when(has[3 if to_upper else 2])
        def _():
            for field in range(2):
                row_copy(field, to_upper).wait_send()

    for side in range(2):

        @pl.when(has[side])
        def _():
            col_copy(side).wait_send()


def finish_kernel(
    adv_ref, edge_w_ref, edge_e_ref, energy_ref, push_ref, u_ref, v_ref, mask_ref,
    out_hbm, u_hbm, v_hbm,
    stage, out_sem, wind_sem,
):
    freqs, dirs, lons, lats = stage.shape
    winds = [
        pltpu.make_async_copy(u_ref, u_hbm, wind_sem.at[0]),
        pltpu.make_async_copy(v_ref, v_hbm, wind_sem.at[1]),
    ]
    for copy in winds:
        copy.start()
    split = direction_split(dirs)
    row_in = iota((lons, lats), 0)
    mask = mask_ref[...].astype(F32)
    energy = energy_ref[...] / (0.2 * freqs * dirs)

    def out_copy(f):
        return pltpu.make_async_copy(stage.at[f], out_hbm.at[f], out_sem.at[f])

    def one(f, carry):
        fraction = f.astype(F32) / (freqs - 1)
        scale = mask / (1.0 + (0.05 + 0.5 * fraction) * energy)
        grow = scale * (0.1 + 0.4 * fraction)
        for d in range(dirs):
            moved = adv_ref[f, d]
            if d < split:
                moved = moved + jnp.where(row_in == 0, edge_w_ref[f, d : d + 1, :], 0.0)
            else:
                moved = moved + jnp.where(row_in == lons - 1, edge_e_ref[f, d - split : d - split + 1, :], 0.0)
            stage[f, d] = moved * (scale + grow * push_ref[d])
        out_copy(f).start()
        return carry

    lax.fori_loop(0, freqs, one, 0)

    def finish(f, carry):
        out_copy(f).wait()
        return carry

    lax.fori_loop(0, freqs, finish, 0)
    for copy in winds:
        copy.wait()


def solution(mesh):
    gx_n, gy_n = mesh.shape["gx"], mesh.shape["gy"]
    vmem = pl.BlockSpec(memory_space=pltpu.VMEM)
    anywhere = pl.BlockSpec(memory_space=pltpu.HBM)

    def per_device(wind_u, wind_v, turbines, rotor_level, block_source, block_weight, spectra, sea_mask):
        freqs, dirs, lons, lats = spectra.shape
        levels, rows, width = wind_u.shape
        split = direction_split(dirs)
        dma = pltpu.SemaphoreType.DMA

        def in_hbm(x):
            return pltpu.with_memory_space_constraint(x, pltpu.HBM)

        handed = pl.pallas_call(
            functools.partial(exchange_kernel, (gx_n, gy_n)),
            out_shape=(
                pltpu.VMEM(spectra.shape, F32),
                pltpu.VMEM((freqs, split, lats), F32),
                pltpu.VMEM((freqs, dirs - split, lats), F32),
                pltpu.VMEM((lons, lats), F32),
                pltpu.VMEM((dirs, lons, lats), F32),
                pltpu.VMEM(wind_u.shape, F32),
                pltpu.VMEM(wind_u.shape, F32),
            ),
            in_specs=[anywhere] * 7,
            out_specs=(vmem,) * 7,
            scratch_shapes=[
                pltpu.VMEM(spectra.shape, F32),
                pltpu.VMEM((freqs, dirs - split, lats), F32),
                pltpu.VMEM((freqs, split, lats), F32),
                pltpu.VMEM((freqs, split, lats), F32),
                pltpu.VMEM((freqs, dirs - split, lats), F32),
                pltpu.VMEM(wind_u.shape, F32),
                pltpu.VMEM(wind_u.shape, F32),
                pltpu.VMEM((rows, width), jnp.int32),
                pltpu.VMEM((rows, width), jnp.int32),
                pltpu.VMEM(block_weight.shape, F32),
                pltpu.SMEM(block_source.shape[::-1], jnp.int32),
                pltpu.VMEM((2, rows, width), F32),
                pltpu.VMEM((2, rows, width), F32),
                pltpu.VMEM((2, 2, levels, width), F32),
                pltpu.VMEM((gy_n, TILE, width), F32),
                pltpu.VMEM((gy_n, TILE, width), F32),
                pltpu.VMEM((2, TILE, width), F32),
                pltpu.VMEM((gy_n, TILE, width), F32),
                pltpu.VMEM((lats, lats), F32),
                pltpu.VMEM((lats, width), F32),
                dma((8,)),
                dma((LOADS,)),
                dma((2, HALO_CUTS)),
                dma((2, HALO_CUTS)),
                dma((2,)),
                dma((2,)),
                dma((2, 2)),
                dma((2, 2)),
                dma((gy_n - 1,)),
                dma((gy_n - 1,)),
                dma((2,)),
                dma((gy_n,)),
            ],
            compiler_params=pltpu.CompilerParams(
                collective_id=0, has_side_effects=True, vmem_limit_bytes=20 * 2**20
            ),
        )(
            in_hbm(wind_u), in_hbm(wind_v), in_hbm(turbines), in_hbm(rotor_level), in_hbm(block_source.T),
            in_hbm(block_weight), in_hbm(spectra),
        )
        adv, edge_w, edge_e, energy, push, u_next, v_next = handed
        spectra_next, u_done, v_done = pl.pallas_call(
            finish_kernel,
            out_shape=(
                jax.ShapeDtypeStruct(spectra.shape, F32),
                jax.ShapeDtypeStruct(wind_u.shape, F32),
                jax.ShapeDtypeStruct(wind_u.shape, F32),
            ),
            in_specs=[vmem] * 8,
            out_specs=(anywhere,) * 3,
            scratch_shapes=[
                pltpu.VMEM(spectra.shape, F32),
                dma((freqs,)),
                dma((2,)),
            ],
            compiler_params=pltpu.CompilerParams(vmem_limit_bytes=20 * 2**20),
        )(adv, edge_w, edge_e, energy, push, u_next, v_next, sea_mask)
        return u_done, v_done, spectra_next

    in_specs = (
        P(None, "gy", "gx"),
        P(None, "gy", "gx"),
        P("gy", "gx"),
        P("gy", "gx"),
        P(),
        P(),
        P(None, None, ("gx", "gy"), None),
        P(("gx", "gy"), None),
    )
    out_specs = (P(None, "gy", "gx"), P(None, "gy", "gx"), P(None, None, ("gx", "gy"), None))
    return jax.shard_map(per_device, mesh=mesh, in_specs=in_specs, out_specs=out_specs, check_vma=False)
```

```python
import functools
import math

import jax
import jax.numpy as jnp
from jax import lax
from jax.experimental import pallas as pl
from jax.experimental.pallas import tpu as pltpu
from jax.sharding import PartitionSpec as P

ROTOR = 3
LOADS = 6
HALO_CUTS = (16, 16, 4)
HOLD_Z = 3
HOLD_D = 2
TILE = 8
MESH = pl.DeviceIdType.MESH
F32 = jnp.float32


def angles(dirs):
    out = []
    for d in range(dirs):
        theta = -math.pi / 2 + (d + 0.5) * (2.0 * math.pi / dirs)
        out.append((math.cos(theta), math.sin(theta)))
    return out


def direction_split(dirs):
    west = [c > 0 for c, _ in angles(dirs)]
    split = sum(west)
    assert all(west[:split]) and not any(west[split:])
    return split


def iota(shape, axis):
    return lax.broadcasted_iota(jnp.int32, shape, axis)


def exchange_kernel(
    sizes,
    u_hbm, v_hbm, turb_hbm, rotor_hbm, source_hbm, weight_hbm, spectra_hbm,
    adv_ref, edge_w_ref, edge_e_ref, energy_ref, push_ref, u_out, v_out,
    x_ref, edge_to_w, edge_to_e, halo_w, halo_e, u_ref, v_ref, turb_ref, rotor_ref, weight_ref, source_ref,
    col_send, col_recv, row_recv, pack_ref, lat_recv, side_send, side_recv, mix_ref, lat_ref,
    load_sem, x_sem, halo_send_sem, halo_recv_sem, col_send_sem, col_recv_sem, row_send_sem, row_recv_sem,
    lat_send_sem, lat_recv_sem, side_send_sem, side_recv_sem,
):
    gx_n, gy_n = sizes
    freqs, dirs, lons, lats = x_ref.shape
    levels, rows, width = u_ref.shape
    split = direction_split(dirs)
    gx, gy = lax.axis_index("gx"), lax.axis_index("gy")
    tile = gx * gy_n + gy
    tiles = gx_n * gy_n
    east = tile + 1
    west = tile - 1
    east_id = (lax.rem(east, tiles) // gy_n, lax.rem(east, gy_n))
    west_id = (lax.rem(west + tiles, tiles) // gy_n, lax.rem(west + tiles, gy_n))
    has_east, has_west = tile < tiles - 1, tile > 0
    has = (gx > 0, gx < gx_n - 1, gy > 0, gy < gy_n - 1)
    side_id = ((gx - 1, gy), (gx + 1, gy), (gx, gy - 1), (gx, gy + 1))
    first, last = gy == 0, gy == gy_n - 1
    assert gy_n > 1 and rows == 2 * TILE and rows * gy_n == lats and lons * gy_n == width

    barrier = pltpu.get_barrier_semaphore()

    def greet(who):
        pl.semaphore_signal(barrier, inc=1, device_id=who, device_id_type=MESH)

    for step in range(1, gy_n):
        greet((gx, lax.rem(gy + step, gy_n)))
    for there, edge, at in ((has[0], first, gx - 1), (has[1], last, gx + 1)):

        @pl.when(there)
        def _():
            greet((at, gy))

        @pl.when(there & edge)
        def _():
            for j in range(gy_n):
                greet((at, j))

    expected = gy_n - 1 + 2 * has[0].astype(jnp.int32) + 2 * has[1].astype(jnp.int32)

    edge_loads = [
        pltpu.make_async_copy(spectra_hbm.at[:, pl.ds(0, split), lons - 1, :], edge_to_e, load_sem.at[6]),
        pltpu.make_async_copy(spectra_hbm.at[:, pl.ds(split, dirs - split), 0, :], edge_to_w, load_sem.at[7]),
    ]
    local = [
        pltpu.make_async_copy(src, dst, load_sem.at[i])
        for i, (src, dst) in enumerate(
            (
                (u_hbm, u_ref), (v_hbm, v_ref), (turb_hbm, turb_ref), (rotor_hbm, rotor_ref),
                (weight_hbm, weight_ref), (source_hbm, source_ref),
            )
        )
    ]
    for copy in local[:4] + edge_loads + local[4:]:
        copy.start()
    per_load = freqs // LOADS

    def load(i):
        part = pl.ds(i * per_load, per_load)
        return pltpu.make_async_copy(spectra_hbm.at[part], x_ref.at[part], x_sem.at[i])

    for i in range(LOADS):
        load(i).start()

    local[0].wait()
    local[1].wait()
    local[2].wait()
    local[3].wait()
    lane = iota((rows, width), 1)
    row = iota((rows, width), 0)
    rate = 0.08 * turb_ref[...].astype(F32)
    lowest = rotor_ref[...]

    def drag_of(level):
        own = (u_ref[level], v_ref[level])
        speed = jnp.sqrt(own[0] * own[0] + own[1] * own[1] + 0.25)
        inside = jnp.where((level >= lowest) & (level < lowest + ROTOR), 1.0, 0.0).astype(F32)
        return 1.0 + rate * inside * speed

    half = width // 2
    span = lons + 2
    assert 2 * span + lons <= half
    lane_t = iota((TILE, width), 1)
    in_half = lax.rem(lane_t, half)
    low = [u_ref[0], v_ref[0], drag_of(0)]

    def turned(x, by):
        by = by % width
        return pltpu.roll(x, by, 1) if by else x

    def halves(shifts):
        out = []
        for h in range(2):
            parts = [turned(x[h * TILE : (h + 1) * TILE], h * half + s) for x, s in zip(low, shifts)]
            block = jnp.where(in_half < span, parts[0], parts[1])
            if len(parts) == 3:
                block = jnp.where(in_half < 2 * span, block, parts[2])
            out.append(block)
        return jnp.where(lane_t < half, out[0], out[1])

    for p in range(gy_n):
        pack_ref[p] = halves((1 - p * lons, span + 1 - p * lons, 2 * span - p * lons))
    side_send[0] = halves((span - 1, 2 * span - 1))
    side_send[1] = halves((1 - width, span + 1 - width))
    lat_recv[gy] = pack_ref[gy]

    for side in range(2):
        at = 0 if side == 0 else width - 1
        packed = jnp.zeros((rows, width), F32)
        for field, ref in enumerate((u_ref, v_ref)):
            for level in range(levels):
                slot = field * levels + level
                packed = jnp.where(lane == slot, pltpu.roll(ref[level], (slot - at) % width, 1), packed)
        col_send[side] = packed

    pl.semaphore_wait(barrier, expected)

    def side_copy(to_east):
        return pltpu.make_async_remote_copy(
            src_ref=side_send.at[int(to_east)],
            dst_ref=side_recv.at[gy],
            send_sem=side_send_sem.at[int(to_east)],
            recv_sem=side_recv_sem.at[gy],
            device_id=(gx + 1, 0) if to_east else (gx - 1, gy_n - 1),
            device_id_type=MESH,
        )

    def side_arrival(j):
        return pltpu.make_async_remote_copy(
            src_ref=side_send.at[0],
            dst_ref=side_recv.at[j],
            send_sem=side_send_sem.at[0],
            recv_sem=side_recv_sem.at[j],
            device_id=east_id,
            device_id_type=MESH,
        )

    def lat_copy(step):
        return pltpu.make_async_remote_copy(
            src_ref=pack_ref.at[lax.rem(gy + step, gy_n)],
            dst_ref=lat_recv.at[gy],
            send_sem=lat_send_sem.at[step - 1],
            recv_sem=lat_recv_sem.at[step - 1],
            device_id=(gx, lax.rem(gy + step, gy_n)),
            device_id_type=MESH,
        )

    def lat_arrival(step):
        return pltpu.make_async_remote_copy(
            src_ref=pack_ref.at[gy],
            dst_ref=lat_recv.at[lax.rem(gy - step + gy_n, gy_n)],
            send_sem=lat_send_sem.at[step - 1],
            recv_sem=lat_recv_sem.at[step - 1],
            device_id=(gx, lax.rem(gy + step, gy_n)),
            device_id_type=MESH,
        )

    def row_copy(field, to_upper):
        ref = (u_ref, v_ref)[field]
        slot = 0 if to_upper else 1
        return pltpu.make_async_remote_copy(
            src_ref=ref.at[:, rows - 1 if to_upper else 0, :],
            dst_ref=row_recv.at[slot, field],
            send_sem=row_send_sem.at[slot, field],
            recv_sem=row_recv_sem.at[slot, field],
            device_id=side_id[3 if to_upper else 2],
            device_id_type=MESH,
        )

    def col_copy(side):
        return pltpu.make_async_remote_copy(
            src_ref=col_send.at[side],
            dst_ref=col_recv.at[1 - side],
            send_sem=col_send_sem.at[side],
            recv_sem=col_recv_sem.at[1 - side],
            device_id=side_id[side],
            device_id_type=MESH,
        )

    assert sum(HALO_CUTS) == freqs
    begins = [sum(HALO_CUTS[:i]) for i in range(len(HALO_CUTS))]
    cuts = range(len(HALO_CUTS))

    def halo_copy(to_east, i):
        part = pl.ds(begins[i], HALO_CUTS[i])
        return pltpu.make_async_remote_copy(
            src_ref=(edge_to_e if to_east else edge_to_w).at[part],
            dst_ref=(halo_w if to_east else halo_e).at[part],
            send_sem=halo_send_sem.at[int(to_east), i],
            recv_sem=halo_recv_sem.at[int(to_east), i],
            device_id=east_id if to_east else west_id,
            device_id_type=MESH,
        )

    neighbours = ((True, has_east), (False, has_west))
    arrivals = ((True, has_west), (False, has_east))
    beyond = ((True, has[1]), (False, has[0]))

    for copy in edge_loads:
        copy.wait()
    far_east, far_west = lax.rem(gy, 4) == 3, lax.rem(gy, 4) == 0
    held = {}
    for to_east, there in neighbours:
        far = far_east if to_east else far_west
        over = last if to_east else first
        if to_east:
            late_d, late_z = there & far & jnp.logical_not(over) & (gx == 0), jnp.bool_(False)
        else:
            late_d, late_z = jnp.bool_(False), there & over & (gx == 1)
        held.setdefault(HOLD_D, []).append((to_east, late_d))
        held.setdefault(HOLD_Z, []).append((to_east, late_z))
        held.setdefault(0, []).append((to_east, there & jnp.logical_not(late_d | late_z)))

    def send_halos(stage, these):
        for to_east, there in held.get(stage, []):

            @pl.when(there)
            def _():
                for i in these:
                    halo_copy(to_east, i).start()

    send_halos(0, cuts[:1])

    for to_east, there in beyond:

        @pl.when(there)
        def _():
            side_copy(to_east).start()

    for step in range(1, gy_n):
        lat_copy(step).start()

    for to_upper in (False, True):

        @pl.when(has[3 if to_upper else 2])
        def _():
            for field in range(2):
                row_copy(field, to_upper).start()

    for side in range(2):

        @pl.when(has[side])
        def _():
            col_copy(side).start()

    send_halos(0, cuts[1:])

    for to_east, there in arrivals:

        @pl.when(jnp.logical_not(there))
        def _():
            halo = halo_w if to_east else halo_e
            halo[...] = jnp.zeros_like(halo)

    for edge, there in ((first, has[0]), (last, has[1])):

        @pl.when(edge & jnp.logical_not(there))
        def _():
            side_recv[...] = jnp.zeros_like(side_recv)

    row_in = iota((lons, lats), 0)
    lane_in = iota((lons, lats), 1)
    keep_w = jnp.where(row_in == 0, 0.0, 1.0).astype(F32)
    keep_e = jnp.where(row_in == lons - 1, 0.0, 1.0).astype(F32)
    keep_s = jnp.where(lane_in == 0, 0.0, 1.0).astype(F32)
    keep_n = jnp.where(lane_in == lats - 1, 0.0, 1.0).astype(F32)
    turns = angles(dirs)

    def advect(f, carry):
        total, courant = carry
        for d, (cos_d, sin_d) in enumerate(turns):
            x = x_ref[f, d]
            a = courant * abs(cos_d)
            b = courant * abs(sin_d)
            if cos_d > 0:
                along = (a * keep_w) * pltpu.roll(x, 1, 0)
            else:
                along = (a * keep_e) * pltpu.roll(x, lons - 1, 0)
            if sin_d > 0:
                across = (b * keep_s) * pltpu.roll(x, 1, 1)
            else:
                across = (b * keep_n) * pltpu.roll(x, lats - 1, 1)
            moved = (1.0 - a - b) * x + along + across
            adv_ref[f, d] = moved
            total = total + moved
        return total, courant * 0.93

    carry = (jnp.zeros((lons, lats), F32), jnp.float32(0.7))
    for i in range(LOADS):
        if i > 0:
            send_halos(i, cuts)
        load(i).wait()
        carry = lax.fori_loop(i * per_load, (i + 1) * per_load, advect, carry)
    total = carry[0]

    local[4].wait()
    local[5].wait()
    blocks, slots = weight_ref.shape[0], weight_ref.shape[1]
    block_of = iota((rows, lats), 1) // rows
    wide, picks = [], []
    for k in range(slots):
        wide.append(jnp.concatenate([weight_ref[b, k] for b in range(blocks)], axis=1))
        pick = jnp.zeros((rows, lats), jnp.int32)
        for b in range(blocks):
            pick = jnp.where(block_of == b, source_ref[k, b], pick)
        picks.append(pick)
    for source in range(blocks):
        part = jnp.zeros((rows, lats), F32)
        for k in range(slots):
            part = part + jnp.where(picks[k] == source, wide[k], 0.0)
        mix_ref[source * rows : (source + 1) * rows, :] = part

    for step in range(1, gy_n):
        lat_arrival(step).wait_recv()
    for edge, there in ((first, has[0]), (last, has[1])):

        @pl.when(edge & there)
        def _():
            for j in range(gy_n):
                side_arrival(j).wait_recv()

    beside = jnp.where(first, 0, jnp.where(last, span - 1, -width))
    from_side = (in_half == beside) | (in_half == beside + span)
    for j in range(gy_n):
        block = jnp.where(from_side, side_recv[j], lat_recv[j])
        lat_ref[j * rows : j * rows + TILE, :] = block
        lat_ref[j * rows + TILE : (j + 1) * rows, :] = pltpu.roll(block, half, 1)
    low_all = lat_ref[...]
    lat_row = iota((lats, width), 0)
    lat_lane = iota((lats, width), 1)
    lower = jnp.where(lat_row == 0, 0.0, pltpu.roll(low_all, 1, 0))
    upper = jnp.where(lat_row == lats - 1, 0.0, pltpu.roll(low_all, lats - 1, 0))
    around = upper + lower + pltpu.roll(low_all, width - 1, 1) + pltpu.roll(low_all, 1, 1) - 4.0 * low_all
    drag_u, drag_v = turned(low_all, 1 - 2 * span), turned(low_all, 1 - span)
    is_u = (lat_lane >= 1) & (lat_lane <= lons)
    is_v = (lat_lane >= span + 1) & (lat_lane <= span + lons)
    low_next = (low_all + 0.2 * around) / jnp.where(is_u, drag_u, jnp.where(is_v, drag_v, 1.0))
    low_v = turned(low_next, -span)
    surface = jnp.sqrt(low_next * low_next + low_v * low_v + 0.25)
    stress = jnp.where(
        lat_lane < lons, turned(surface * low_next, -1),
        jnp.where(lat_lane < 2 * lons, turned(surface * low_v, lons - 1), 0.0),
    )
    wave = lax.dot_general(
        stress, mix_ref[...], (((0,), (0,)), ((), ())),
        precision=lax.Precision.HIGHEST, preferred_element_type=F32,
    )
    wave_x, wave_y = wave[0:lons], wave[lons : 2 * lons]
    for d, (cos_d, sin_d) in enumerate(turns):
        push_ref[d] = jnp.maximum(0.0, wave_x * cos_d + wave_y * sin_d)

    for side in range(2):

        @pl.when(has[side])
        def _():
            col_copy(1 - side).wait_recv()

        @pl.when(jnp.logical_not(has[side]))
        def _():
            col_recv[side] = jnp.zeros((rows, width), F32)

        @pl.when(has[2 + side])
        def _():
            for field in range(2):
                row_copy(field, side == 0).wait_recv()

        @pl.when(jnp.logical_not(has[2 + side]))
        def _():
            row_recv[side] = jnp.zeros_like(row_recv[side])

    for level in range(levels):
        drag = drag_of(level)
        for field, (ref, out) in enumerate(((u_ref, u_out), (v_ref, v_out))):
            x = ref[level]
            slot = field * levels + level
            down = jnp.where(row == 0, row_recv[0, field, level : level + 1, :], pltpu.roll(x, 1, 0))
            up = jnp.where(row == rows - 1, row_recv[1, field, level : level + 1, :], pltpu.roll(x, rows - 1, 0))
            left = jnp.where(lane == 0, pltpu.roll(col_recv[0], (0 - slot) % width, 1), pltpu.roll(x, 1, 1))
            right = jnp.where(
                lane == width - 1, pltpu.roll(col_recv[1], (width - 1 - slot) % width, 1), pltpu.roll(x, width - 1, 1)
            )
            out[level] = (x + 0.2 * (up + down + right + left - 4.0 * x)) / drag

    def turn(count, begin):
        theta = -math.pi / 2 + (iota((count, lats), 0).astype(F32) + (begin + 0.5)) * (2.0 * math.pi / dirs)
        return jnp.abs(jnp.cos(theta))

    turn_w, turn_e = turn(split, 0), turn(dirs - split, split)

    def edges(f, carry):
        acc_w, acc_e, courant = carry
        value_w = (courant * turn_w) * halo_w[f]
        value_e = (courant * turn_e) * halo_e[f]
        edge_w_ref[f] = value_w
        edge_e_ref[f] = value_e
        return acc_w + value_w, acc_e + value_e, courant * 0.93

    sums = (jnp.zeros((split, lats), F32), jnp.zeros((dirs - split, lats), F32), jnp.float32(0.7))
    for i in cuts:
        for to_east, there in arrivals:

            @pl.when(there)
            def _():
                halo_copy(to_east, i).wait_recv()

        sums = lax.fori_loop(begins[i], begins[i] + HALO_CUTS[i], edges, sums)
    sum_w = jnp.sum(sums[0], axis=0, keepdims=True)
    sum_e = jnp.sum(sums[1], axis=0, keepdims=True)
    energy_ref[...] = total + jnp.where(row_in == 0, sum_w, 0.0) + jnp.where(row_in == lons - 1, sum_e, 0.0)

    for to_east, there in beyond:

        @pl.when(there)
        def _():
            side_copy(to_east).wait_send()

    for to_east, there in neighbours:

        @pl.when(there)
        def _():
            for i in cuts:
                halo_copy(to_east, i).wait_send()

    for step in range(1, gy_n):
        lat_copy(step).wait_send()

    for to_upper in (False, True):

        @pl.when(has[3 if to_upper else 2])
        def _():
            for field in range(2):
                row_copy(field, to_upper).wait_send()

    for side in range(2):

        @pl.when(has[side])
        def _():
            col_copy(side).wait_send()


def finish_kernel(
    adv_ref, edge_w_ref, edge_e_ref, energy_ref, push_ref, u_ref, v_ref, mask_ref,
    out_hbm, u_hbm, v_hbm,
    stage, out_sem, wind_sem,
):
    freqs, dirs, lons, lats = stage.shape
    winds = [
        pltpu.make_async_copy(u_ref, u_hbm, wind_sem.at[0]),
        pltpu.make_async_copy(v_ref, v_hbm, wind_sem.at[1]),
    ]
    for copy in winds:
        copy.start()
    split = direction_split(dirs)
    row_in = iota((lons, lats), 0)
    mask = mask_ref[...].astype(F32)
    energy = energy_ref[...] / (0.2 * freqs * dirs)

    def out_copy(f):
        return pltpu.make_async_copy(stage.at[f], out_hbm.at[f], out_sem.at[f])

    def one(f, carry):
        fraction = f.astype(F32) / (freqs - 1)
        scale = mask / (1.0 + (0.05 + 0.5 * fraction) * energy)
        grow = scale * (0.1 + 0.4 * fraction)
        for d in range(dirs):
            moved = adv_ref[f, d]
            if d < split:
                moved = moved + jnp.where(row_in == 0, edge_w_ref[f, d : d + 1, :], 0.0)
            else:
                moved = moved + jnp.where(row_in == lons - 1, edge_e_ref[f, d - split : d - split + 1, :], 0.0)
            stage[f, d] = moved * (scale + grow * push_ref[d])
        out_copy(f).start()
        return carry

    lax.fori_loop(0, freqs, one, 0)

    def finish(f, carry):
        out_copy(f).wait()
        return carry

    lax.fori_loop(0, freqs, finish, 0)
    for copy in winds:
        copy.wait()


def solution(mesh):
    gx_n, gy_n = mesh.shape["gx"], mesh.shape["gy"]
    vmem = pl.BlockSpec(memory_space=pltpu.VMEM)
    anywhere = pl.BlockSpec(memory_space=pltpu.HBM)

    def per_device(wind_u, wind_v, turbines, rotor_level, block_source, block_weight, spectra, sea_mask):
        freqs, dirs, lons, lats = spectra.shape
        levels, rows, width = wind_u.shape
        split = direction_split(dirs)
        dma = pltpu.SemaphoreType.DMA

        def in_hbm(x):
            return pltpu.with_memory_space_constraint(x, pltpu.HBM)

        handed = pl.pallas_call(
            functools.partial(exchange_kernel, (gx_n, gy_n)),
            out_shape=(
                pltpu.VMEM(spectra.shape, F32),
                pltpu.VMEM((freqs, split, lats), F32),
                pltpu.VMEM((freqs, dirs - split, lats), F32),
                pltpu.VMEM((lons, lats), F32),
                pltpu.VMEM((dirs, lons, lats), F32),
                pltpu.VMEM(wind_u.shape, F32),
                pltpu.VMEM(wind_u.shape, F32),
            ),
            in_specs=[anywhere] * 7,
            out_specs=(vmem,) * 7,
            scratch_shapes=[
                pltpu.VMEM(spectra.shape, F32),
                pltpu.VMEM((freqs, dirs - split, lats), F32),
                pltpu.VMEM((freqs, split, lats), F32),
                pltpu.VMEM((freqs, split, lats), F32),
                pltpu.VMEM((freqs, dirs - split, lats), F32),
                pltpu.VMEM(wind_u.shape, F32),
                pltpu.VMEM(wind_u.shape, F32),
                pltpu.VMEM((rows, width), jnp.int32),
                pltpu.VMEM((rows, width), jnp.int32),
                pltpu.VMEM(block_weight.shape, F32),
                pltpu.SMEM(block_source.shape[::-1], jnp.int32),
                pltpu.VMEM((2, rows, width), F32),
                pltpu.VMEM((2, rows, width), F32),
                pltpu.VMEM((2, 2, levels, width), F32),
                pltpu.VMEM((gy_n, TILE, width), F32),
                pltpu.VMEM((gy_n, TILE, width), F32),
                pltpu.VMEM((2, TILE, width), F32),
                pltpu.VMEM((gy_n, TILE, width), F32),
                pltpu.VMEM((lats, lats), F32),
                pltpu.VMEM((lats, width), F32),
                dma((8,)),
                dma((LOADS,)),
                dma((2, len(HALO_CUTS))),
                dma((2, len(HALO_CUTS))),
                dma((2,)),
                dma((2,)),
                dma((2, 2)),
                dma((2, 2)),
                dma((gy_n - 1,)),
                dma((gy_n - 1,)),
                dma((2,)),
                dma((gy_n,)),
            ],
            compiler_params=pltpu.CompilerParams(
                collective_id=0, has_side_effects=True, vmem_limit_bytes=20 * 2**20
            ),
        )(
            in_hbm(wind_u), in_hbm(wind_v), in_hbm(turbines), in_hbm(rotor_level), in_hbm(block_source.T),
            in_hbm(block_weight), in_hbm(spectra),
        )
        adv, edge_w, edge_e, energy, push, u_next, v_next = handed
        spectra_next, u_done, v_done = pl.pallas_call(
            finish_kernel,
            out_shape=(
                jax.ShapeDtypeStruct(spectra.shape, F32),
                jax.ShapeDtypeStruct(wind_u.shape, F32),
                jax.ShapeDtypeStruct(wind_u.shape, F32),
            ),
            in_specs=[vmem] * 8,
            out_specs=(anywhere,) * 3,
            scratch_shapes=[
                pltpu.VMEM(spectra.shape, F32),
                dma((freqs,)),
                dma((2,)),
            ],
            compiler_params=pltpu.CompilerParams(vmem_limit_bytes=20 * 2**20),
        )(adv, edge_w, edge_e, energy, push, u_next, v_next, sea_mask)
        return u_done, v_done, spectra_next

    in_specs = (
        P(None, "gy", "gx"),
        P(None, "gy", "gx"),
        P("gy", "gx"),
        P("gy", "gx"),
        P(),
        P(),
        P(None, None, ("gx", "gy"), None),
        P(("gx", "gy"), None),
    )
    out_specs = (P(None, "gy", "gx"), P(None, "gy", "gx"), P(None, None, ("gx", "gy"), None))
    return jax.shard_map(per_device, mesh=mesh, in_specs=in_specs, out_specs=out_specs, check_vma=False)
```

```python
import functools
import math

import jax
import jax.numpy as jnp
from jax import lax
from jax.experimental import pallas as pl
from jax.experimental.pallas import tpu as pltpu
from jax.sharding import PartitionSpec as P

ROTOR = 3
LOADS = 6
HALO_CUTS = (8, 24, 4)
HOLD_Z = 4
HOLD_D = 3
TILE = 8
MESH = pl.DeviceIdType.MESH
F32 = jnp.float32


def angles(dirs):
    out = []
    for d in range(dirs):
        theta = -math.pi / 2 + (d + 0.5) * (2.0 * math.pi / dirs)
        out.append((math.cos(theta), math.sin(theta)))
    return out


def direction_split(dirs):
    west = [c > 0 for c, _ in angles(dirs)]
    split = sum(west)
    assert all(west[:split]) and not any(west[split:])
    return split


def iota(shape, axis):
    return lax.broadcasted_iota(jnp.int32, shape, axis)


def exchange_kernel(
    sizes,
    u_hbm, v_hbm, turb_hbm, rotor_hbm, source_hbm, weight_hbm, spectra_hbm,
    adv_ref, edge_w_ref, edge_e_ref, energy_ref, push_ref, u_out, v_out,
    x_ref, edge_to_w, edge_to_e, halo_w, halo_e, u_ref, v_ref, turb_ref, rotor_ref, weight_ref, source_ref,
    col_send, col_recv, row_recv, pack_ref, lat_recv, side_send, side_recv, mix_ref, lat_ref,
    load_sem, x_sem, halo_send_sem, halo_recv_sem, col_send_sem, col_recv_sem, row_send_sem, row_recv_sem,
    lat_send_sem, lat_recv_sem, side_send_sem, side_recv_sem,
):
    gx_n, gy_n = sizes
    freqs, dirs, lons, lats = x_ref.shape
    levels, rows, width = u_ref.shape
    split = direction_split(dirs)
    gx, gy = lax.axis_index("gx"), lax.axis_index("gy")
    tile = gx * gy_n + gy
    tiles = gx_n * gy_n
    east = tile + 1
    west = tile - 1
    east_id = (lax.rem(east, tiles) // gy_n, lax.rem(east, gy_n))
    west_id = (lax.rem(west + tiles, tiles) // gy_n, lax.rem(west + tiles, gy_n))
    has_east, has_west = tile < tiles - 1, tile > 0
    has = (gx > 0, gx < gx_n - 1, gy > 0, gy < gy_n - 1)
    side_id = ((gx - 1, gy), (gx + 1, gy), (gx, gy - 1), (gx, gy + 1))
    first, last = gy == 0, gy == gy_n - 1
    assert gy_n > 1 and rows == 2 * TILE and rows * gy_n == lats and lons * gy_n == width

    barrier = pltpu.get_barrier_semaphore()

    def greet(who):
        pl.semaphore_signal(barrier, inc=1, device_id=who, device_id_type=MESH)

    for step in range(1, gy_n):
        greet((gx, lax.rem(gy + step, gy_n)))
    for there, edge, at in ((has[0], first, gx - 1), (has[1], last, gx + 1)):

        @pl.when(there)
        def _():
            greet((at, gy))

        @pl.when(there & edge)
        def _():
            for j in range(gy_n):
                greet((at, j))

    expected = gy_n - 1 + 2 * has[0].astype(jnp.int32) + 2 * has[1].astype(jnp.int32)

    edge_loads = [
        pltpu.make_async_copy(spectra_hbm.at[:, pl.ds(0, split), lons - 1, :], edge_to_e, load_sem.at[6]),
        pltpu.make_async_copy(spectra_hbm.at[:, pl.ds(split, dirs - split), 0, :], edge_to_w, load_sem.at[7]),
    ]
    local = [
        pltpu.make_async_copy(src, dst, load_sem.at[i])
        for i, (src, dst) in enumerate(
            (
                (u_hbm, u_ref), (v_hbm, v_ref), (turb_hbm, turb_ref), (rotor_hbm, rotor_ref),
                (weight_hbm, weight_ref), (source_hbm, source_ref),
            )
        )
    ]
    for copy in local[:4] + edge_loads + local[4:]:
        copy.start()
    per_load = freqs // LOADS

    def load(i):
        part = pl.ds(i * per_load, per_load)
        return pltpu.make_async_copy(spectra_hbm.at[part], x_ref.at[part], x_sem.at[i])

    for i in range(LOADS):
        load(i).start()

    local[0].wait()
    local[1].wait()
    local[2].wait()
    local[3].wait()
    lane = iota((rows, width), 1)
    row = iota((rows, width), 0)
    rate = 0.08 * turb_ref[...].astype(F32)
    lowest = rotor_ref[...]

    def drag_of(level):
        own = (u_ref[level], v_ref[level])
        speed = jnp.sqrt(own[0] * own[0] + own[1] * own[1] + 0.25)
        inside = jnp.where((level >= lowest) & (level < lowest + ROTOR), 1.0, 0.0).astype(F32)
        return 1.0 + rate * inside * speed

    half = width // 2
    span = lons + 2
    assert 2 * span + lons <= half
    lane_t = iota((TILE, width), 1)
    in_half = lax.rem(lane_t, half)
    low = [u_ref[0], v_ref[0], drag_of(0)]

    def turned(x, by):
        by = by % width
        return pltpu.roll(x, by, 1) if by else x

    def halves(shifts):
        out = []
        for h in range(2):
            parts = [turned(x[h * TILE : (h + 1) * TILE], h * half + s) for x, s in zip(low, shifts)]
            block = jnp.where(in_half < span, parts[0], parts[1])
            if len(parts) == 3:
                block = jnp.where(in_half < 2 * span, block, parts[2])
            out.append(block)
        return jnp.where(lane_t < half, out[0], out[1])

    for p in range(gy_n):
        pack_ref[p] = halves((1 - p * lons, span + 1 - p * lons, 2 * span - p * lons))
    side_send[0] = halves((span - 1, 2 * span - 1))
    side_send[1] = halves((1 - width, span + 1 - width))
    lat_recv[gy] = pack_ref[gy]

    for side in range(2):
        at = 0 if side == 0 else width - 1
        packed = jnp.zeros((rows, width), F32)
        for field, ref in enumerate((u_ref, v_ref)):
            for level in range(levels):
                slot = field * levels + level
                packed = jnp.where(lane == slot, pltpu.roll(ref[level], (slot - at) % width, 1), packed)
        col_send[side] = packed

    pl.semaphore_wait(barrier, expected)

    def side_copy(to_east):
        return pltpu.make_async_remote_copy(
            src_ref=side_send.at[int(to_east)],
            dst_ref=side_recv.at[gy],
            send_sem=side_send_sem.at[int(to_east)],
            recv_sem=side_recv_sem.at[gy],
            device_id=(gx + 1, 0) if to_east else (gx - 1, gy_n - 1),
            device_id_type=MESH,
        )

    def side_arrival(j):
        return pltpu.make_async_remote_copy(
            src_ref=side_send.at[0],
            dst_ref=side_recv.at[j],
            send_sem=side_send_sem.at[0],
            recv_sem=side_recv_sem.at[j],
            device_id=east_id,
            device_id_type=MESH,
        )

    def lat_copy(step):
        return pltpu.make_async_remote_copy(
            src_ref=pack_ref.at[lax.rem(gy + step, gy_n)],
            dst_ref=lat_recv.at[gy],
            send_sem=lat_send_sem.at[step - 1],
            recv_sem=lat_recv_sem.at[step - 1],
            device_id=(gx, lax.rem(gy + step, gy_n)),
            device_id_type=MESH,
        )

    def lat_arrival(step):
        return pltpu.make_async_remote_copy(
            src_ref=pack_ref.at[gy],
            dst_ref=lat_recv.at[lax.rem(gy - step + gy_n, gy_n)],
            send_sem=lat_send_sem.at[step - 1],
            recv_sem=lat_recv_sem.at[step - 1],
            device_id=(gx, lax.rem(gy + step, gy_n)),
            device_id_type=MESH,
        )

    def row_copy(field, to_upper):
        ref = (u_ref, v_ref)[field]
        slot = 0 if to_upper else 1
        return pltpu.make_async_remote_copy(
            src_ref=ref.at[:, rows - 1 if to_upper else 0, :],
            dst_ref=row_recv.at[slot, field],
            send_sem=row_send_sem.at[slot, field],
            recv_sem=row_recv_sem.at[slot, field],
            device_id=side_id[3 if to_upper else 2],
            device_id_type=MESH,
        )

    def col_copy(side):
        return pltpu.make_async_remote_copy(
            src_ref=col_send.at[side],
            dst_ref=col_recv.at[1 - side],
            send_sem=col_send_sem.at[side],
            recv_sem=col_recv_sem.at[1 - side],
            device_id=side_id[side],
            device_id_type=MESH,
        )

    assert sum(HALO_CUTS) == freqs
    begins = [sum(HALO_CUTS[:i]) for i in range(len(HALO_CUTS))]
    cuts = range(len(HALO_CUTS))

    def halo_copy(to_east, i):
        part = pl.ds(begins[i], HALO_CUTS[i])
        return pltpu.make_async_remote_copy(
            src_ref=(edge_to_e if to_east else edge_to_w).at[part],
            dst_ref=(halo_w if to_east else halo_e).at[part],
            send_sem=halo_send_sem.at[int(to_east), i],
            recv_sem=halo_recv_sem.at[int(to_east), i],
            device_id=east_id if to_east else west_id,
            device_id_type=MESH,
        )

    neighbours = ((True, has_east), (False, has_west))
    arrivals = ((True, has_west), (False, has_east))
    beyond = ((True, has[1]), (False, has[0]))

    for copy in edge_loads:
        copy.wait()
    far_east, far_west = lax.rem(gy, 4) == 3, lax.rem(gy, 4) == 0
    held = {}
    for to_east, there in neighbours:
        far = far_east if to_east else far_west
        over = last if to_east else first
        if to_east:
            late_d, late_z = there & far & jnp.logical_not(over) & (gx == 0), jnp.bool_(False)
        else:
            late_d, late_z = jnp.bool_(False), there & over & (gx == 1)
        held.setdefault(HOLD_D, []).append((to_east, late_d))
        held.setdefault(HOLD_Z, []).append((to_east, late_z))
        held.setdefault(0, []).append((to_east, there & jnp.logical_not(late_d | late_z)))

    def send_halos(stage, these):
        for to_east, there in held.get(stage, []):

            @pl.when(there)
            def _():
                for i in these:
                    halo_copy(to_east, i).start()

    for to_east, there in neighbours:

        @pl.when(there)
        def _():
            halo_copy(to_east, 0).start()

    for to_east, there in beyond:

        @pl.when(there)
        def _():
            side_copy(to_east).start()

    for step in range(1, gy_n):
        lat_copy(step).start()

    for to_upper in (False, True):

        @pl.when(has[3 if to_upper else 2])
        def _():
            for field in range(2):
                row_copy(field, to_upper).start()

    for side in range(2):

        @pl.when(has[side])
        def _():
            col_copy(side).start()

    send_halos(0, cuts[1:])

    for to_east, there in arrivals:

        @pl.when(jnp.logical_not(there))
        def _():
            halo = halo_w if to_east else halo_e
            halo[...] = jnp.zeros_like(halo)

    for edge, there in ((first, has[0]), (last, has[1])):

        @pl.when(edge & jnp.logical_not(there))
        def _():
            side_recv[...] = jnp.zeros_like(side_recv)

    row_in = iota((lons, lats), 0)
    lane_in = iota((lons, lats), 1)
    keep_w = jnp.where(row_in == 0, 0.0, 1.0).astype(F32)
    keep_e = jnp.where(row_in == lons - 1, 0.0, 1.0).astype(F32)
    keep_s = jnp.where(lane_in == 0, 0.0, 1.0).astype(F32)
    keep_n = jnp.where(lane_in == lats - 1, 0.0, 1.0).astype(F32)
    turns = angles(dirs)

    def advect(f, carry):
        total, courant = carry
        for d, (cos_d, sin_d) in enumerate(turns):
            x = x_ref[f, d]
            a = courant * abs(cos_d)
            b = courant * abs(sin_d)
            if cos_d > 0:
                along = (a * keep_w) * pltpu.roll(x, 1, 0)
            else:
                along = (a * keep_e) * pltpu.roll(x, lons - 1, 0)
            if sin_d > 0:
                across = (b * keep_s) * pltpu.roll(x, 1, 1)
            else:
                across = (b * keep_n) * pltpu.roll(x, lats - 1, 1)
            moved = (1.0 - a - b) * x + along + across
            adv_ref[f, d] = moved
            total = total + moved
        return total, courant * 0.93

    carry = (jnp.zeros((lons, lats), F32), jnp.float32(0.7))
    for i in range(LOADS):
        if i > 0:
            send_halos(i, cuts[1:])
        load(i).wait()
        carry = lax.fori_loop(i * per_load, (i + 1) * per_load, advect, carry)
    total = carry[0]

    local[4].wait()
    local[5].wait()
    blocks, slots = weight_ref.shape[0], weight_ref.shape[1]
    block_of = iota((rows, lats), 1) // rows
    wide, picks = [], []
    for k in range(slots):
        wide.append(jnp.concatenate([weight_ref[b, k] for b in range(blocks)], axis=1))
        pick = jnp.zeros((rows, lats), jnp.int32)
        for b in range(blocks):
            pick = jnp.where(block_of == b, source_ref[k, b], pick)
        picks.append(pick)
    for source in range(blocks):
        part = jnp.zeros((rows, lats), F32)
        for k in range(slots):
            part = part + jnp.where(picks[k] == source, wide[k], 0.0)
        mix_ref[source * rows : (source + 1) * rows, :] = part

    for step in range(1, gy_n):
        lat_arrival(step).wait_recv()
    for edge, there in ((first, has[0]), (last, has[1])):

        @pl.when(edge & there)
        def _():
            for j in range(gy_n):
                side_arrival(j).wait_recv()

    beside = jnp.where(first, 0, jnp.where(last, span - 1, -width))
    from_side = (in_half == beside) | (in_half == beside + span)
    for j in range(gy_n):
        block = jnp.where(from_side, side_recv[j], lat_recv[j])
        lat_ref[j * rows : j * rows + TILE, :] = block
        lat_ref[j * rows + TILE : (j + 1) * rows, :] = pltpu.roll(block, half, 1)
    low_all = lat_ref[...]
    lat_row = iota((lats, width), 0)
    lat_lane = iota((lats, width), 1)
    lower = jnp.where(lat_row == 0, 0.0, pltpu.roll(low_all, 1, 0))
    upper = jnp.where(lat_row == lats - 1, 0.0, pltpu.roll(low_all, lats - 1, 0))
    around = upper + lower + pltpu.roll(low_all, width - 1, 1) + pltpu.roll(low_all, 1, 1) - 4.0 * low_all
    drag_u, drag_v = turned(low_all, 1 - 2 * span), turned(low_all, 1 - span)
    is_u = (lat_lane >= 1) & (lat_lane <= lons)
    is_v = (lat_lane >= span + 1) & (lat_lane <= span + lons)
    low_next = (low_all + 0.2 * around) / jnp.where(is_u, drag_u, jnp.where(is_v, drag_v, 1.0))
    low_v = turned(low_next, -span)
    surface = jnp.sqrt(low_next * low_next + low_v * low_v + 0.25)
    stress = jnp.where(
        lat_lane < lons, turned(surface * low_next, -1),
        jnp.where(lat_lane < 2 * lons, turned(surface * low_v, lons - 1), 0.0),
    )
    wave = lax.dot_general(
        stress, mix_ref[...], (((0,), (0,)), ((), ())),
        precision=lax.Precision.HIGHEST, preferred_element_type=F32,
    )
    wave_x, wave_y = wave[0:lons], wave[lons : 2 * lons]
    for d, (cos_d, sin_d) in enumerate(turns):
        push_ref[d] = jnp.maximum(0.0, wave_x * cos_d + wave_y * sin_d)

    for side in range(2):

        @pl.when(has[side])
        def _():
            col_copy(1 - side).wait_recv()

        @pl.when(jnp.logical_not(has[side]))
        def _():
            col_recv[side] = jnp.zeros((rows, width), F32)

        @pl.when(has[2 + side])
        def _():
            for field in range(2):
                row_copy(field, side == 0).wait_recv()

        @pl.when(jnp.logical_not(has[2 + side]))
        def _():
            row_recv[side] = jnp.zeros_like(row_recv[side])

    for level in range(levels):
        drag = drag_of(level)
        for field, (ref, out) in enumerate(((u_ref, u_out), (v_ref, v_out))):
            x = ref[level]
            slot = field * levels + level
            down = jnp.where(row == 0, row_recv[0, field, level : level + 1, :], pltpu.roll(x, 1, 0))
            up = jnp.where(row == rows - 1, row_recv[1, field, level : level + 1, :], pltpu.roll(x, rows - 1, 0))
            left = jnp.where(lane == 0, pltpu.roll(col_recv[0], (0 - slot) % width, 1), pltpu.roll(x, 1, 1))
            right = jnp.where(
                lane == width - 1, pltpu.roll(col_recv[1], (width - 1 - slot) % width, 1), pltpu.roll(x, width - 1, 1)
            )
            out[level] = (x + 0.2 * (up + down + right + left - 4.0 * x)) / drag

    def turn(count, begin):
        theta = -math.pi / 2 + (iota((count, lats), 0).astype(F32) + (begin + 0.5)) * (2.0 * math.pi / dirs)
        return jnp.abs(jnp.cos(theta))

    turn_w, turn_e = turn(split, 0), turn(dirs - split, split)

    def edges(f, carry):
        acc_w, acc_e, courant = carry
        value_w = (courant * turn_w) * halo_w[f]
        value_e = (courant * turn_e) * halo_e[f]
        edge_w_ref[f] = value_w
        edge_e_ref[f] = value_e
        return acc_w + value_w, acc_e + value_e, courant * 0.93

    sums = (jnp.zeros((split, lats), F32), jnp.zeros((dirs - split, lats), F32), jnp.float32(0.7))
    for i in cuts:
        if i == cuts[-1]:
            for to_east, there in beyond:

                @pl.when(there)
                def _():
                    side_copy(to_east).wait_send()

            for to_east, there in neighbours:

                @pl.when(there)
                def _():
                    for k in cuts[:-1]:
                        halo_copy(to_east, k).wait_send()

            for step in range(1, gy_n):
                lat_copy(step).wait_send()

            for to_upper in (False, True):

                @pl.when(has[3 if to_upper else 2])
                def _():
                    for field in range(2):
                        row_copy(field, to_upper).wait_send()

            for side in range(2):

                @pl.when(has[side])
                def _():
                    col_copy(side).wait_send()

        for to_east, there in arrivals:

            @pl.when(there)
            def _():
                halo_copy(to_east, i).wait_recv()

        sums = lax.fori_loop(begins[i], begins[i] + HALO_CUTS[i], edges, sums)
    sum_w = jnp.sum(sums[0], axis=0, keepdims=True)
    sum_e = jnp.sum(sums[1], axis=0, keepdims=True)
    energy_ref[...] = total + jnp.where(row_in == 0, sum_w, 0.0) + jnp.where(row_in == lons - 1, sum_e, 0.0)
    for to_east, there in neighbours:

        @pl.when(there)
        def _():
            halo_copy(to_east, cuts[-1]).wait_send()


def finish_kernel(
    adv_ref, edge_w_ref, edge_e_ref, energy_ref, push_ref, u_ref, v_ref, mask_ref,
    out_hbm, u_hbm, v_hbm,
    stage, out_sem, wind_sem,
):
    freqs, dirs, lons, lats = stage.shape
    winds = [
        pltpu.make_async_copy(u_ref, u_hbm, wind_sem.at[0]),
        pltpu.make_async_copy(v_ref, v_hbm, wind_sem.at[1]),
    ]
    for copy in winds:
        copy.start()
    split = direction_split(dirs)
    row_in = iota((lons, lats), 0)
    mask = mask_ref[...].astype(F32)
    energy = energy_ref[...] / (0.2 * freqs * dirs)

    def out_copy(f):
        return pltpu.make_async_copy(stage.at[f], out_hbm.at[f], out_sem.at[f])

    def one(f, carry):
        fraction = f.astype(F32) / (freqs - 1)
        scale = mask / (1.0 + (0.05 + 0.5 * fraction) * energy)
        grow = scale * (0.1 + 0.4 * fraction)
        for d in range(dirs):
            moved = adv_ref[f, d]
            if d < split:
                moved = moved + jnp.where(row_in == 0, edge_w_ref[f, d : d + 1, :], 0.0)
            else:
                moved = moved + jnp.where(row_in == lons - 1, edge_e_ref[f, d - split : d - split + 1, :], 0.0)
            stage[f, d] = moved * (scale + grow * push_ref[d])
        out_copy(f).start()
        return carry

    lax.fori_loop(0, freqs, one, 0)

    def finish(f, carry):
        out_copy(f).wait()
        return carry

    lax.fori_loop(0, freqs, finish, 0)
    for copy in winds:
        copy.wait()


def solution(mesh):
    gx_n, gy_n = mesh.shape["gx"], mesh.shape["gy"]
    vmem = pl.BlockSpec(memory_space=pltpu.VMEM)
    anywhere = pl.BlockSpec(memory_space=pltpu.HBM)

    def per_device(wind_u, wind_v, turbines, rotor_level, block_source, block_weight, spectra, sea_mask):
        freqs, dirs, lons, lats = spectra.shape
        levels, rows, width = wind_u.shape
        split = direction_split(dirs)
        dma = pltpu.SemaphoreType.DMA

        def in_hbm(x):
            return pltpu.with_memory_space_constraint(x, pltpu.HBM)

        handed = pl.pallas_call(
            functools.partial(exchange_kernel, (gx_n, gy_n)),
            out_shape=(
                pltpu.VMEM(spectra.shape, F32),
                pltpu.VMEM((freqs, split, lats), F32),
                pltpu.VMEM((freqs, dirs - split, lats), F32),
                pltpu.VMEM((lons, lats), F32),
                pltpu.VMEM((dirs, lons, lats), F32),
                pltpu.VMEM(wind_u.shape, F32),
                pltpu.VMEM(wind_u.shape, F32),
            ),
            in_specs=[anywhere] * 7,
            out_specs=(vmem,) * 7,
            scratch_shapes=[
                pltpu.VMEM(spectra.shape, F32),
                pltpu.VMEM((freqs, dirs - split, lats), F32),
                pltpu.VMEM((freqs, split, lats), F32),
                pltpu.VMEM((freqs, split, lats), F32),
                pltpu.VMEM((freqs, dirs - split, lats), F32),
                pltpu.VMEM(wind_u.shape, F32),
                pltpu.VMEM(wind_u.shape, F32),
                pltpu.VMEM((rows, width), jnp.int32),
                pltpu.VMEM((rows, width), jnp.int32),
                pltpu.VMEM(block_weight.shape, F32),
                pltpu.SMEM(block_source.shape[::-1], jnp.int32),
                pltpu.VMEM((2, rows, width), F32),
                pltpu.VMEM((2, rows, width), F32),
                pltpu.VMEM((2, 2, levels, width), F32),
                pltpu.VMEM((gy_n, TILE, width), F32),
                pltpu.VMEM((gy_n, TILE, width), F32),
                pltpu.VMEM((2, TILE, width), F32),
                pltpu.VMEM((gy_n, TILE, width), F32),
                pltpu.VMEM((lats, lats), F32),
                pltpu.VMEM((lats, width), F32),
                dma((8,)),
                dma((LOADS,)),
                dma((2, len(HALO_CUTS))),
                dma((2, len(HALO_CUTS))),
                dma((2,)),
                dma((2,)),
                dma((2, 2)),
                dma((2, 2)),
                dma((gy_n - 1,)),
                dma((gy_n - 1,)),
                dma((2,)),
                dma((gy_n,)),
            ],
            compiler_params=pltpu.CompilerParams(
                collective_id=0, has_side_effects=True, vmem_limit_bytes=20 * 2**20
            ),
        )(
            in_hbm(wind_u), in_hbm(wind_v), in_hbm(turbines), in_hbm(rotor_level), in_hbm(block_source.T),
            in_hbm(block_weight), in_hbm(spectra),
        )
        adv, edge_w, edge_e, energy, push, u_next, v_next = handed
        spectra_next, u_done, v_done = pl.pallas_call(
            finish_kernel,
            out_shape=(
                jax.ShapeDtypeStruct(spectra.shape, F32),
                jax.ShapeDtypeStruct(wind_u.shape, F32),
                jax.ShapeDtypeStruct(wind_u.shape, F32),
            ),
            in_specs=[vmem] * 8,
            out_specs=(anywhere,) * 3,
            scratch_shapes=[
                pltpu.VMEM(spectra.shape, F32),
                dma((freqs,)),
                dma((2,)),
            ],
            compiler_params=pltpu.CompilerParams(vmem_limit_bytes=20 * 2**20),
        )(adv, edge_w, edge_e, energy, push, u_next, v_next, sea_mask)
        return u_done, v_done, spectra_next

    in_specs = (
        P(None, "gy", "gx"),
        P(None, "gy", "gx"),
        P("gy", "gx"),
        P("gy", "gx"),
        P(),
        P(),
        P(None, None, ("gx", "gy"), None),
        P(("gx", "gy"), None),
    )
    out_specs = (P(None, "gy", "gx"), P(None, "gy", "gx"), P(None, None, ("gx", "gy"), None))
    return jax.shard_map(per_device, mesh=mesh, in_specs=in_specs, out_specs=out_specs, check_vma=False)
```

```python
import functools
import math

import jax
import jax.numpy as jnp
from jax import lax
from jax.experimental import pallas as pl
from jax.experimental.pallas import tpu as pltpu
from jax.sharding import PartitionSpec as P

ROTOR = 3
LOADS = 6
HALO_CUTS = (8, 24, 4)
HOLD_Z = 4
HOLD_D = 4
TILE = 8
MESH = pl.DeviceIdType.MESH
F32 = jnp.float32


def angles(dirs):
    out = []
    for d in range(dirs):
        theta = -math.pi / 2 + (d + 0.5) * (2.0 * math.pi / dirs)
        out.append((math.cos(theta), math.sin(theta)))
    return out


def direction_split(dirs):
    west = [c > 0 for c, _ in angles(dirs)]
    split = sum(west)
    assert all(west[:split]) and not any(west[split:])
    return split


def iota(shape, axis):
    return lax.broadcasted_iota(jnp.int32, shape, axis)


def exchange_kernel(
    sizes,
    u_hbm, v_hbm, turb_hbm, rotor_hbm, source_hbm, weight_hbm, spectra_hbm,
    adv_ref, edge_w_ref, edge_e_ref, energy_ref, push_ref, u_out, v_out,
    x_ref, edge_to_w, edge_to_e, halo_w, halo_e, u_ref, v_ref, turb_ref, rotor_ref, weight_ref, source_ref,
    col_send, col_recv, row_recv, pack_ref, lat_recv, side_send, side_recv, mix_ref, lat_ref,
    load_sem, x_sem, halo_send_sem, halo_recv_sem, col_send_sem, col_recv_sem, row_send_sem, row_recv_sem,
    lat_send_sem, lat_recv_sem, side_send_sem, side_recv_sem,
):
    gx_n, gy_n = sizes
    freqs, dirs, lons, lats = x_ref.shape
    levels, rows, width = u_ref.shape
    split = direction_split(dirs)
    gx, gy = lax.axis_index("gx"), lax.axis_index("gy")
    tile = gx * gy_n + gy
    tiles = gx_n * gy_n
    east = tile + 1
    west = tile - 1
    east_id = (lax.rem(east, tiles) // gy_n, lax.rem(east, gy_n))
    west_id = (lax.rem(west + tiles, tiles) // gy_n, lax.rem(west + tiles, gy_n))
    has_east, has_west = tile < tiles - 1, tile > 0
    has = (gx > 0, gx < gx_n - 1, gy > 0, gy < gy_n - 1)
    side_id = ((gx - 1, gy), (gx + 1, gy), (gx, gy - 1), (gx, gy + 1))
    first, last = gy == 0, gy == gy_n - 1
    assert gy_n > 1 and rows == 2 * TILE and rows * gy_n == lats and lons * gy_n == width

    barrier = pltpu.get_barrier_semaphore()

    def greet(who):
        pl.semaphore_signal(barrier, inc=1, device_id=who, device_id_type=MESH)

    for step in range(1, gy_n):
        greet((gx, lax.rem(gy + step, gy_n)))
    for there, edge, at in ((has[0], first, gx - 1), (has[1], last, gx + 1)):

        @pl.when(there)
        def _():
            greet((at, gy))

        @pl.when(there & edge)
        def _():
            for j in range(gy_n):
                greet((at, j))

    expected = gy_n - 1 + 2 * has[0].astype(jnp.int32) + 2 * has[1].astype(jnp.int32)

    edge_loads = [
        pltpu.make_async_copy(spectra_hbm.at[:, pl.ds(0, split), lons - 1, :], edge_to_e, load_sem.at[6]),
        pltpu.make_async_copy(spectra_hbm.at[:, pl.ds(split, dirs - split), 0, :], edge_to_w, load_sem.at[7]),
    ]
    local = [
        pltpu.make_async_copy(src, dst, load_sem.at[i])
        for i, (src, dst) in enumerate(
            (
                (u_hbm, u_ref), (v_hbm, v_ref), (turb_hbm, turb_ref), (rotor_hbm, rotor_ref),
                (weight_hbm, weight_ref), (source_hbm, source_ref),
            )
        )
    ]
    for copy in local[:4] + edge_loads + local[4:]:
        copy.start()
    per_load = freqs // LOADS

    def load(i):
        part = pl.ds(i * per_load, per_load)
        return pltpu.make_async_copy(spectra_hbm.at[part], x_ref.at[part], x_sem.at[i])

    for i in range(LOADS):
        load(i).start()

    local[0].wait()
    local[1].wait()
    local[2].wait()
    local[3].wait()
    lane = iota((rows, width), 1)
    row = iota((rows, width), 0)
    rate = 0.08 * turb_ref[...].astype(F32)
    lowest = rotor_ref[...]

    def drag_of(level):
        own = (u_ref[level], v_ref[level])
        speed = jnp.sqrt(own[0] * own[0] + own[1] * own[1] + 0.25)
        inside = jnp.where((level >= lowest) & (level < lowest + ROTOR), 1.0, 0.0).astype(F32)
        return 1.0 + rate * inside * speed

    half = width // 2
    span = lons + 2
    assert 2 * span + lons <= half
    lane_t = iota((TILE, width), 1)
    in_half = lax.rem(lane_t, half)
    low = [u_ref[0], v_ref[0], drag_of(0)]

    def turned(x, by):
        by = by % width
        return pltpu.roll(x, by, 1) if by else x

    def halves(shifts):
        out = []
        for h in range(2):
            parts = [turned(x[h * TILE : (h + 1) * TILE], h * half + s) for x, s in zip(low, shifts)]
            block = jnp.where(in_half < span, parts[0], parts[1])
            if len(parts) == 3:
                block = jnp.where(in_half < 2 * span, block, parts[2])
            out.append(block)
        return jnp.where(lane_t < half, out[0], out[1])

    for p in range(gy_n):
        pack_ref[p] = halves((1 - p * lons, span + 1 - p * lons, 2 * span - p * lons))
    side_send[0] = halves((span - 1, 2 * span - 1))
    side_send[1] = halves((1 - width, span + 1 - width))
    lat_recv[gy] = pack_ref[gy]

    for side in range(2):
        at = 0 if side == 0 else width - 1
        packed = jnp.zeros((rows, width), F32)
        for field, ref in enumerate((u_ref, v_ref)):
            for level in range(levels):
                slot = field * levels + level
                packed = jnp.where(lane == slot, pltpu.roll(ref[level], (slot - at) % width, 1), packed)
        col_send[side] = packed

    pl.semaphore_wait(barrier, expected)

    def side_copy(to_east):
        return pltpu.make_async_remote_copy(
            src_ref=side_send.at[int(to_east)],
            dst_ref=side_recv.at[gy],
            send_sem=side_send_sem.at[int(to_east)],
            recv_sem=side_recv_sem.at[gy],
            device_id=(gx + 1, 0) if to_east else (gx - 1, gy_n - 1),
            device_id_type=MESH,
        )

    def side_arrival(j):
        return pltpu.make_async_remote_copy(
            src_ref=side_send.at[0],
            dst_ref=side_recv.at[j],
            send_sem=side_send_sem.at[0],
            recv_sem=side_recv_sem.at[j],
            device_id=east_id,
            device_id_type=MESH,
        )

    def lat_copy(step):
        return pltpu.make_async_remote_copy(
            src_ref=pack_ref.at[lax.rem(gy + step, gy_n)],
            dst_ref=lat_recv.at[gy],
            send_sem=lat_send_sem.at[step - 1],
            recv_sem=lat_recv_sem.at[step - 1],
            device_id=(gx, lax.rem(gy + step, gy_n)),
            device_id_type=MESH,
        )

    def lat_arrival(step):
        return pltpu.make_async_remote_copy(
            src_ref=pack_ref.at[gy],
            dst_ref=lat_recv.at[lax.rem(gy - step + gy_n, gy_n)],
            send_sem=lat_send_sem.at[step - 1],
            recv_sem=lat_recv_sem.at[step - 1],
            device_id=(gx, lax.rem(gy + step, gy_n)),
            device_id_type=MESH,
        )

    def row_copy(field, to_upper):
        ref = (u_ref, v_ref)[field]
        slot = 0 if to_upper else 1
        return pltpu.make_async_remote_copy(
            src_ref=ref.at[:, rows - 1 if to_upper else 0, :],
            dst_ref=row_recv.at[slot, field],
            send_sem=row_send_sem.at[slot, field],
            recv_sem=row_recv_sem.at[slot, field],
            device_id=side_id[3 if to_upper else 2],
            device_id_type=MESH,
        )

    def col_copy(side):
        return pltpu.make_async_remote_copy(
            src_ref=col_send.at[side],
            dst_ref=col_recv.at[1 - side],
            send_sem=col_send_sem.at[side],
            recv_sem=col_recv_sem.at[1 - side],
            device_id=side_id[side],
            device_id_type=MESH,
        )

    assert sum(HALO_CUTS) == freqs
    begins = [sum(HALO_CUTS[:i]) for i in range(len(HALO_CUTS))]
    cuts = range(len(HALO_CUTS))

    def halo_copy(to_east, i):
        part = pl.ds(begins[i], HALO_CUTS[i])
        return pltpu.make_async_remote_copy(
            src_ref=(edge_to_e if to_east else edge_to_w).at[part],
            dst_ref=(halo_w if to_east else halo_e).at[part],
            send_sem=halo_send_sem.at[int(to_east), i],
            recv_sem=halo_recv_sem.at[int(to_east), i],
            device_id=east_id if to_east else west_id,
            device_id_type=MESH,
        )

    neighbours = ((True, has_east), (False, has_west))
    arrivals = ((True, has_west), (False, has_east))
    beyond = ((True, has[1]), (False, has[0]))

    for copy in edge_loads:
        copy.wait()
    far_east, far_west = lax.rem(gy, 4) == 3, lax.rem(gy, 4) == 0
    held = {}
    for to_east, there in neighbours:
        far = far_east if to_east else far_west
        over = last if to_east else first
        if to_east:
            late_d, late_z = there & far & jnp.logical_not(over) & (gx == 0), jnp.bool_(False)
        else:
            late_d, late_z = jnp.bool_(False), there & over & (gx == 1)
        held.setdefault(HOLD_D, []).append((to_east, late_d))
        held.setdefault(HOLD_Z, []).append((to_east, late_z))
        held.setdefault(0, []).append((to_east, there & jnp.logical_not(late_d | late_z)))

    def send_halos(stage, these):
        for to_east, there in held.get(stage, []):

            @pl.when(there)
            def _():
                for i in these:
                    halo_copy(to_east, i).start()

    for to_east, there in neighbours:

        @pl.when(there)
        def _():
            halo_copy(to_east, 0).start()

    for to_east, there in beyond:

        @pl.when(there)
        def _():
            side_copy(to_east).start()

    for step in range(1, gy_n):
        lat_copy(step).start()

    for to_upper in (False, True):

        @pl.when(has[3 if to_upper else 2])
        def _():
            for field in range(2):
                row_copy(field, to_upper).start()

    for side in range(2):

        @pl.when(has[side])
        def _():
            col_copy(side).start()

    send_halos(0, cuts[1:])

    for to_east, there in arrivals:

        @pl.when(jnp.logical_not(there))
        def _():
            halo = halo_w if to_east else halo_e
            halo[...] = jnp.zeros_like(halo)

    for edge, there in ((first, has[0]), (last, has[1])):

        @pl.when(edge & jnp.logical_not(there))
        def _():
            side_recv[...] = jnp.zeros_like(side_recv)

    row_in = iota((lons, lats), 0)
    lane_in = iota((lons, lats), 1)
    keep_w = jnp.where(row_in == 0, 0.0, 1.0).astype(F32)
    keep_e = jnp.where(row_in == lons - 1, 0.0, 1.0).astype(F32)
    keep_s = jnp.where(lane_in == 0, 0.0, 1.0).astype(F32)
    keep_n = jnp.where(lane_in == lats - 1, 0.0, 1.0).astype(F32)
    turns = angles(dirs)

    def advect(f, carry):
        total, courant = carry
        for d, (cos_d, sin_d) in enumerate(turns):
            x = x_ref[f, d]
            a = courant * abs(cos_d)
            b = courant * abs(sin_d)
            if cos_d > 0:
                along = (a * keep_w) * pltpu.roll(x, 1, 0)
            else:
                along = (a * keep_e) * pltpu.roll(x, lons - 1, 0)
            if sin_d > 0:
                across = (b * keep_s) * pltpu.roll(x, 1, 1)
            else:
                across = (b * keep_n) * pltpu.roll(x, lats - 1, 1)
            moved = (1.0 - a - b) * x + along + across
            adv_ref[f, d] = moved
            total = total + moved
        return total, courant * 0.93

    carry = (jnp.zeros((lons, lats), F32), jnp.float32(0.7))
    for i in range(LOADS):
        if i > 0:
            send_halos(i, cuts[1:])
        load(i).wait()
        carry = lax.fori_loop(i * per_load, (i + 1) * per_load, advect, carry)
    total = carry[0]

    local[4].wait()
    local[5].wait()
    blocks, slots = weight_ref.shape[0], weight_ref.shape[1]
    block_of = iota((rows, lats), 1) // rows
    wide, picks = [], []
    for k in range(slots):
        wide.append(jnp.concatenate([weight_ref[b, k] for b in range(blocks)], axis=1))
        pick = jnp.zeros((rows, lats), jnp.int32)
        for b in range(blocks):
            pick = jnp.where(block_of == b, source_ref[k, b], pick)
        picks.append(pick)
    for source in range(blocks):
        part = jnp.zeros((rows, lats), F32)
        for k in range(slots):
            part = part + jnp.where(picks[k] == source, wide[k], 0.0)
        mix_ref[source * rows : (source + 1) * rows, :] = part

    for step in range(1, gy_n):
        lat_arrival(step).wait_recv()
    for edge, there in ((first, has[0]), (last, has[1])):

        @pl.when(edge & there)
        def _():
            for j in range(gy_n):
                side_arrival(j).wait_recv()

    beside = jnp.where(first, 0, jnp.where(last, span - 1, -width))
    from_side = (in_half == beside) | (in_half == beside + span)
    for j in range(gy_n):
        block = jnp.where(from_side, side_recv[j], lat_recv[j])
        lat_ref[j * rows : j * rows + TILE, :] = block
        lat_ref[j * rows + TILE : (j + 1) * rows, :] = pltpu.roll(block, half, 1)
    low_all = lat_ref[...]
    lat_row = iota((lats, width), 0)
    lat_lane = iota((lats, width), 1)
    lower = jnp.where(lat_row == 0, 0.0, pltpu.roll(low_all, 1, 0))
    upper = jnp.where(lat_row == lats - 1, 0.0, pltpu.roll(low_all, lats - 1, 0))
    around = upper + lower + pltpu.roll(low_all, width - 1, 1) + pltpu.roll(low_all, 1, 1) - 4.0 * low_all
    drag_u, drag_v = turned(low_all, 1 - 2 * span), turned(low_all, 1 - span)
    is_u = (lat_lane >= 1) & (lat_lane <= lons)
    is_v = (lat_lane >= span + 1) & (lat_lane <= span + lons)
    low_next = (low_all + 0.2 * around) / jnp.where(is_u, drag_u, jnp.where(is_v, drag_v, 1.0))
    low_v = turned(low_next, -span)
    surface = jnp.sqrt(low_next * low_next + low_v * low_v + 0.25)
    stress = jnp.where(
        lat_lane < lons, turned(surface * low_next, -1),
        jnp.where(lat_lane < 2 * lons, turned(surface * low_v, lons - 1), 0.0),
    )
    wave = lax.dot_general(
        stress, mix_ref[...], (((0,), (0,)), ((), ())),
        precision=lax.Precision.HIGHEST, preferred_element_type=F32,
    )
    wave_x, wave_y = wave[0:lons], wave[lons : 2 * lons]
    for d, (cos_d, sin_d) in enumerate(turns):
        push_ref[d] = jnp.maximum(0.0, wave_x * cos_d + wave_y * sin_d)

    for side in range(2):

        @pl.when(has[side])
        def _():
            col_copy(1 - side).wait_recv()

        @pl.when(jnp.logical_not(has[side]))
        def _():
            col_recv[side] = jnp.zeros((rows, width), F32)

        @pl.when(has[2 + side])
        def _():
            for field in range(2):
                row_copy(field, side == 0).wait_recv()

        @pl.when(jnp.logical_not(has[2 + side]))
        def _():
            row_recv[side] = jnp.zeros_like(row_recv[side])

    for level in range(levels):
        drag = drag_of(level)
        for field, (ref, out) in enumerate(((u_ref, u_out), (v_ref, v_out))):
            x = ref[level]
            slot = field * levels + level
            down = jnp.where(row == 0, row_recv[0, field, level : level + 1, :], pltpu.roll(x, 1, 0))
            up = jnp.where(row == rows - 1, row_recv[1, field, level : level + 1, :], pltpu.roll(x, rows - 1, 0))
            left = jnp.where(lane == 0, pltpu.roll(col_recv[0], (0 - slot) % width, 1), pltpu.roll(x, 1, 1))
            right = jnp.where(
                lane == width - 1, pltpu.roll(col_recv[1], (width - 1 - slot) % width, 1), pltpu.roll(x, width - 1, 1)
            )
            out[level] = (x + 0.2 * (up + down + right + left - 4.0 * x)) / drag

    def turn(count, begin):
        theta = -math.pi / 2 + (iota((count, lats), 0).astype(F32) + (begin + 0.5)) * (2.0 * math.pi / dirs)
        return jnp.abs(jnp.cos(theta))

    turn_w, turn_e = turn(split, 0), turn(dirs - split, split)

    def edges(f, carry):
        acc_w, acc_e, courant = carry
        value_w = (courant * turn_w) * halo_w[f]
        value_e = (courant * turn_e) * halo_e[f]
        edge_w_ref[f] = value_w
        edge_e_ref[f] = value_e
        return acc_w + value_w, acc_e + value_e, courant * 0.93

    sums = (jnp.zeros((split, lats), F32), jnp.zeros((dirs - split, lats), F32), jnp.float32(0.7))
    for i in cuts:
        if i == cuts[-1]:
            for to_east, there in beyond:

                @pl.when(there)
                def _():
                    side_copy(to_east).wait_send()

            for to_east, there in neighbours:

                @pl.when(there)
                def _():
                    for k in cuts[:-1]:
                        halo_copy(to_east, k).wait_send()

            for step in range(1, gy_n):
                lat_copy(step).wait_send()

            for to_upper in (False, True):

                @pl.when(has[3 if to_upper else 2])
                def _():
                    for field in range(2):
                        row_copy(field, to_upper).wait_send()

            for side in range(2):

                @pl.when(has[side])
                def _():
                    col_copy(side).wait_send()

        for to_east, there in arrivals:

            @pl.when(there)
            def _():
                halo_copy(to_east, i).wait_recv()

        sums = lax.fori_loop(begins[i], begins[i] + HALO_CUTS[i], edges, sums, unroll=4)
    sum_w = jnp.sum(sums[0], axis=0, keepdims=True)
    sum_e = jnp.sum(sums[1], axis=0, keepdims=True)
    energy_ref[...] = total + jnp.where(row_in == 0, sum_w, 0.0) + jnp.where(row_in == lons - 1, sum_e, 0.0)
    for to_east, there in neighbours:

        @pl.when(there)
        def _():
            halo_copy(to_east, cuts[-1]).wait_send()


def finish_kernel(
    adv_ref, edge_w_ref, edge_e_ref, energy_ref, push_ref, u_ref, v_ref, mask_ref,
    out_hbm, u_hbm, v_hbm,
    stage, out_sem, wind_sem,
):
    freqs, dirs, lons, lats = stage.shape
    winds = [
        pltpu.make_async_copy(u_ref, u_hbm, wind_sem.at[0]),
        pltpu.make_async_copy(v_ref, v_hbm, wind_sem.at[1]),
    ]
    for copy in winds:
        copy.start()
    split = direction_split(dirs)
    row_in = iota((lons, lats), 0)
    mask = mask_ref[...].astype(F32)
    energy = energy_ref[...] / (0.2 * freqs * dirs)

    def out_copy(f):
        return pltpu.make_async_copy(stage.at[f], out_hbm.at[f], out_sem.at[f])

    def one(f, carry):
        fraction = f.astype(F32) / (freqs - 1)
        scale = mask / (1.0 + (0.05 + 0.5 * fraction) * energy)
        grow = scale * (0.1 + 0.4 * fraction)
        for d in range(dirs):
            moved = adv_ref[f, d]
            if d < split:
                moved = moved + jnp.where(row_in == 0, edge_w_ref[f, d : d + 1, :], 0.0)
            else:
                moved = moved + jnp.where(row_in == lons - 1, edge_e_ref[f, d - split : d - split + 1, :], 0.0)
            stage[f, d] = moved * (scale + grow * push_ref[d])
        out_copy(f).start()
        return carry

    lax.fori_loop(0, freqs, one, 0)

    def finish(f, carry):
        out_copy(f).wait()
        return carry

    lax.fori_loop(0, freqs, finish, 0)
    for copy in winds:
        copy.wait()


def solution(mesh):
    gx_n, gy_n = mesh.shape["gx"], mesh.shape["gy"]
    vmem = pl.BlockSpec(memory_space=pltpu.VMEM)
    anywhere = pl.BlockSpec(memory_space=pltpu.HBM)

    def per_device(wind_u, wind_v, turbines, rotor_level, block_source, block_weight, spectra, sea_mask):
        freqs, dirs, lons, lats = spectra.shape
        levels, rows, width = wind_u.shape
        split = direction_split(dirs)
        dma = pltpu.SemaphoreType.DMA

        def in_hbm(x):
            return pltpu.with_memory_space_constraint(x, pltpu.HBM)

        handed = pl.pallas_call(
            functools.partial(exchange_kernel, (gx_n, gy_n)),
            out_shape=(
                pltpu.VMEM(spectra.shape, F32),
                pltpu.VMEM((freqs, split, lats), F32),
                pltpu.VMEM((freqs, dirs - split, lats), F32),
                pltpu.VMEM((lons, lats), F32),
                pltpu.VMEM((dirs, lons, lats), F32),
                pltpu.VMEM(wind_u.shape, F32),
                pltpu.VMEM(wind_u.shape, F32),
            ),
            in_specs=[anywhere] * 7,
            out_specs=(vmem,) * 7,
            scratch_shapes=[
                pltpu.VMEM(spectra.shape, F32),
                pltpu.VMEM((freqs, dirs - split, lats), F32),
                pltpu.VMEM((freqs, split, lats), F32),
                pltpu.VMEM((freqs, split, lats), F32),
                pltpu.VMEM((freqs, dirs - split, lats), F32),
                pltpu.VMEM(wind_u.shape, F32),
                pltpu.VMEM(wind_u.shape, F32),
                pltpu.VMEM((rows, width), jnp.int32),
                pltpu.VMEM((rows, width), jnp.int32),
                pltpu.VMEM(block_weight.shape, F32),
                pltpu.SMEM(block_source.shape[::-1], jnp.int32),
                pltpu.VMEM((2, rows, width), F32),
                pltpu.VMEM((2, rows, width), F32),
                pltpu.VMEM((2, 2, levels, width), F32),
                pltpu.VMEM((gy_n, TILE, width), F32),
                pltpu.VMEM((gy_n, TILE, width), F32),
                pltpu.VMEM((2, TILE, width), F32),
                pltpu.VMEM((gy_n, TILE, width), F32),
                pltpu.VMEM((lats, lats), F32),
                pltpu.VMEM((lats, width), F32),
                dma((8,)),
                dma((LOADS,)),
                dma((2, len(HALO_CUTS))),
                dma((2, len(HALO_CUTS))),
                dma((2,)),
                dma((2,)),
                dma((2, 2)),
                dma((2, 2)),
                dma((gy_n - 1,)),
                dma((gy_n - 1,)),
                dma((2,)),
                dma((gy_n,)),
            ],
            compiler_params=pltpu.CompilerParams(
                collective_id=0, has_side_effects=True, vmem_limit_bytes=20 * 2**20
            ),
        )(
            in_hbm(wind_u), in_hbm(wind_v), in_hbm(turbines), in_hbm(rotor_level), in_hbm(block_source.T),
            in_hbm(block_weight), in_hbm(spectra),
        )
        adv, edge_w, edge_e, energy, push, u_next, v_next = handed
        spectra_next, u_done, v_done = pl.pallas_call(
            finish_kernel,
            out_shape=(
                jax.ShapeDtypeStruct(spectra.shape, F32),
                jax.ShapeDtypeStruct(wind_u.shape, F32),
                jax.ShapeDtypeStruct(wind_u.shape, F32),
            ),
            in_specs=[vmem] * 8,
            out_specs=(anywhere,) * 3,
            scratch_shapes=[
                pltpu.VMEM(spectra.shape, F32),
                dma((freqs,)),
                dma((2,)),
            ],
            compiler_params=pltpu.CompilerParams(vmem_limit_bytes=20 * 2**20),
        )(adv, edge_w, edge_e, energy, push, u_next, v_next, sea_mask)
        return u_done, v_done, spectra_next

    in_specs = (
        P(None, "gy", "gx"),
        P(None, "gy", "gx"),
        P("gy", "gx"),
        P("gy", "gx"),
        P(),
        P(),
        P(None, None, ("gx", "gy"), None),
        P(("gx", "gy"), None),
    )
    out_specs = (P(None, "gy", "gx"), P(None, "gy", "gx"), P(None, None, ("gx", "gy"), None))
    return jax.shard_map(per_device, mesh=mesh, in_specs=in_specs, out_specs=out_specs, check_vma=False)
```

```python
import functools
import math

import jax
import jax.numpy as jnp
from jax import lax
from jax.experimental import pallas as pl
from jax.experimental.pallas import tpu as pltpu
from jax.sharding import PartitionSpec as P

ROTOR = 3
LOADS = 6
HALO_CUTS = (8, 24, 4)
HOLD_Z = 4
HOLD_D = 3
TILE = 8
MESH = pl.DeviceIdType.MESH
F32 = jnp.float32


def angles(dirs):
    out = []
    for d in range(dirs):
        theta = -math.pi / 2 + (d + 0.5) * (2.0 * math.pi / dirs)
        out.append((math.cos(theta), math.sin(theta)))
    return out


def direction_split(dirs):
    west = [c > 0 for c, _ in angles(dirs)]
    split = sum(west)
    assert all(west[:split]) and not any(west[split:])
    return split


def iota(shape, axis):
    return lax.broadcasted_iota(jnp.int32, shape, axis)


def exchange_kernel(
    sizes,
    u_hbm, v_hbm, turb_hbm, rotor_hbm, source_hbm, weight_hbm, spectra_hbm,
    adv_ref, edge_w_ref, edge_e_ref, energy_ref, push_ref, u_out, v_out,
    x_ref, edge_to_w, edge_to_e, halo_w, halo_e, u_ref, v_ref, turb_ref, rotor_ref, weight_ref, source_ref,
    col_send, col_recv, row_recv, pack_ref, lat_recv, side_send, side_recv, mix_ref, lat_ref,
    load_sem, x_sem, halo_send_sem, halo_recv_sem, col_send_sem, col_recv_sem, row_send_sem, row_recv_sem,
    lat_send_sem, lat_recv_sem, side_send_sem, side_recv_sem,
):
    gx_n, gy_n = sizes
    freqs, dirs, lons, lats = x_ref.shape
    levels, rows, width = u_ref.shape
    split = direction_split(dirs)
    gx, gy = lax.axis_index("gx"), lax.axis_index("gy")
    tile = gx * gy_n + gy
    tiles = gx_n * gy_n
    east = tile + 1
    west = tile - 1
    east_id = (lax.rem(east, tiles) // gy_n, lax.rem(east, gy_n))
    west_id = (lax.rem(west + tiles, tiles) // gy_n, lax.rem(west + tiles, gy_n))
    has_east, has_west = tile < tiles - 1, tile > 0
    has = (gx > 0, gx < gx_n - 1, gy > 0, gy < gy_n - 1)
    side_id = ((gx - 1, gy), (gx + 1, gy), (gx, gy - 1), (gx, gy + 1))
    first, last = gy == 0, gy == gy_n - 1
    assert gy_n > 1 and rows == 2 * TILE and rows * gy_n == lats and lons * gy_n == width

    barrier = pltpu.get_barrier_semaphore()

    def greet(who):
        pl.semaphore_signal(barrier, inc=1, device_id=who, device_id_type=MESH)

    for step in range(1, gy_n):
        greet((gx, lax.rem(gy + step, gy_n)))
    for there, edge, at in ((has[0], first, gx - 1), (has[1], last, gx + 1)):

        @pl.when(there)
        def _():
            greet((at, gy))

        @pl.when(there & edge)
        def _():
            for j in range(gy_n):
                greet((at, j))

    expected = gy_n - 1 + 2 * has[0].astype(jnp.int32) + 2 * has[1].astype(jnp.int32)

    edge_loads = [
        pltpu.make_async_copy(spectra_hbm.at[:, pl.ds(0, split), lons - 1, :], edge_to_e, load_sem.at[6]),
        pltpu.make_async_copy(spectra_hbm.at[:, pl.ds(split, dirs - split), 0, :], edge_to_w, load_sem.at[7]),
    ]
    local = [
        pltpu.make_async_copy(src, dst, load_sem.at[i])
        for i, (src, dst) in enumerate(
            (
                (u_hbm, u_ref), (v_hbm, v_ref), (turb_hbm, turb_ref), (rotor_hbm, rotor_ref),
                (weight_hbm, weight_ref), (source_hbm, source_ref),
            )
        )
    ]
    for copy in local[:4] + edge_loads + local[4:]:
        copy.start()
    per_load = freqs // LOADS

    def load(i):
        part = pl.ds(i * per_load, per_load)
        return pltpu.make_async_copy(spectra_hbm.at[part], x_ref.at[part], x_sem.at[i])

    for i in range(LOADS):
        load(i).start()

    local[0].wait()
    local[1].wait()
    local[2].wait()
    local[3].wait()
    lane = iota((rows, width), 1)
    row = iota((rows, width), 0)
    rate = 0.08 * turb_ref[...].astype(F32)
    lowest = rotor_ref[...]

    def drag_of(level):
        own = (u_ref[level], v_ref[level])
        speed = jnp.sqrt(own[0] * own[0] + own[1] * own[1] + 0.25)
        inside = jnp.where((level >= lowest) & (level < lowest + ROTOR), 1.0, 0.0).astype(F32)
        return 1.0 + rate * inside * speed

    half = width // 2
    span = lons + 2
    assert 2 * span + lons <= half
    lane_t = iota((TILE, width), 1)
    in_half = lax.rem(lane_t, half)
    low = [u_ref[0], v_ref[0], drag_of(0)]

    def turned(x, by):
        by = by % width
        return pltpu.roll(x, by, 1) if by else x

    def halves(shifts):
        out = []
        for h in range(2):
            parts = [turned(x[h * TILE : (h + 1) * TILE], h * half + s) for x, s in zip(low, shifts)]
            block = jnp.where(in_half < span, parts[0], parts[1])
            if len(parts) == 3:
                block = jnp.where(in_half < 2 * span, block, parts[2])
            out.append(block)
        return jnp.where(lane_t < half, out[0], out[1])

    for p in range(gy_n):
        pack_ref[p] = halves((1 - p * lons, span + 1 - p * lons, 2 * span - p * lons))
    side_send[0] = halves((span - 1, 2 * span - 1))
    side_send[1] = halves((1 - width, span + 1 - width))
    lat_recv[gy] = pack_ref[gy]

    for side in range(2):
        at = 0 if side == 0 else width - 1
        packed = jnp.zeros((rows, width), F32)
        for field, ref in enumerate((u_ref, v_ref)):
            for level in range(levels):
                slot = field * levels + level
                packed = jnp.where(lane == slot, pltpu.roll(ref[level], (slot - at) % width, 1), packed)
        col_send[side] = packed

    pl.semaphore_wait(barrier, expected)

    def side_copy(to_east):
        return pltpu.make_async_remote_copy(
            src_ref=side_send.at[int(to_east)],
            dst_ref=side_recv.at[gy],
            send_sem=side_send_sem.at[int(to_east)],
            recv_sem=side_recv_sem.at[gy],
            device_id=(gx + 1, 0) if to_east else (gx - 1, gy_n - 1),
            device_id_type=MESH,
        )

    def side_arrival(j):
        return pltpu.make_async_remote_copy(
            src_ref=side_send.at[0],
            dst_ref=side_recv.at[j],
            send_sem=side_send_sem.at[0],
            recv_sem=side_recv_sem.at[j],
            device_id=east_id,
            device_id_type=MESH,
        )

    def lat_copy(step):
        return pltpu.make_async_remote_copy(
            src_ref=pack_ref.at[lax.rem(gy + step, gy_n)],
            dst_ref=lat_recv.at[gy],
            send_sem=lat_send_sem.at[step - 1],
            recv_sem=lat_recv_sem.at[step - 1],
            device_id=(gx, lax.rem(gy + step, gy_n)),
            device_id_type=MESH,
        )

    def lat_arrival(step):
        return pltpu.make_async_remote_copy(
            src_ref=pack_ref.at[gy],
            dst_ref=lat_recv.at[lax.rem(gy - step + gy_n, gy_n)],
            send_sem=lat_send_sem.at[step - 1],
            recv_sem=lat_recv_sem.at[step - 1],
            device_id=(gx, lax.rem(gy + step, gy_n)),
            device_id_type=MESH,
        )

    def row_copy(field, to_upper):
        ref = (u_ref, v_ref)[field]
        slot = 0 if to_upper else 1
        return pltpu.make_async_remote_copy(
            src_ref=ref.at[:, rows - 1 if to_upper else 0, :],
            dst_ref=row_recv.at[slot, field],
            send_sem=row_send_sem.at[slot, field],
            recv_sem=row_recv_sem.at[slot, field],
            device_id=side_id[3 if to_upper else 2],
            device_id_type=MESH,
        )

    def col_copy(side):
        return pltpu.make_async_remote_copy(
            src_ref=col_send.at[side],
            dst_ref=col_recv.at[1 - side],
            send_sem=col_send_sem.at[side],
            recv_sem=col_recv_sem.at[1 - side],
            device_id=side_id[side],
            device_id_type=MESH,
        )

    assert sum(HALO_CUTS) == freqs
    begins = [sum(HALO_CUTS[:i]) for i in range(len(HALO_CUTS))]
    cuts = range(len(HALO_CUTS))

    def halo_copy(to_east, i):
        part = pl.ds(begins[i], HALO_CUTS[i])
        return pltpu.make_async_remote_copy(
            src_ref=(edge_to_e if to_east else edge_to_w).at[part],
            dst_ref=(halo_w if to_east else halo_e).at[part],
            send_sem=halo_send_sem.at[int(to_east), i],
            recv_sem=halo_recv_sem.at[int(to_east), i],
            device_id=east_id if to_east else west_id,
            device_id_type=MESH,
        )

    neighbours = ((True, has_east), (False, has_west))
    arrivals = ((True, has_west), (False, has_east))
    beyond = ((True, has[1]), (False, has[0]))

    for copy in edge_loads:
        copy.wait()
    far_east, far_west = lax.rem(gy, 4) == 3, lax.rem(gy, 4) == 0
    held = {}
    for to_east, there in neighbours:
        far = far_east if to_east else far_west
        over = last if to_east else first
        if to_east:
            late_d, late_z = there & far & jnp.logical_not(over) & (gx == 0), jnp.bool_(False)
        else:
            late_d, late_z = jnp.bool_(False), there & over & (gx == 1)
        held.setdefault(HOLD_D, []).append((to_east, late_d))
        held.setdefault(HOLD_Z, []).append((to_east, late_z))
        held.setdefault(0, []).append((to_east, there & jnp.logical_not(late_d | late_z)))

    def send_halos(stage, these):
        for to_east, there in held.get(stage, []):

            @pl.when(there)
            def _():
                for i in these:
                    halo_copy(to_east, i).start()

    for to_east, there in neighbours:

        @pl.when(there)
        def _():
            halo_copy(to_east, 0).start()

    for to_east, there in beyond:

        @pl.when(there)
        def _():
            side_copy(to_east).start()

    for step in range(1, gy_n):
        lat_copy(step).start()

    for to_upper in (False, True):

        @pl.when(has[3 if to_upper else 2])
        def _():
            for field in range(2):
                row_copy(field, to_upper).start()

    for side in range(2):

        @pl.when(has[side])
        def _():
            col_copy(side).start()

    send_halos(0, cuts[1:])

    for to_east, there in arrivals:

        @pl.when(jnp.logical_not(there))
        def _():
            halo = halo_w if to_east else halo_e
            halo[...] = jnp.zeros_like(halo)

    for edge, there in ((first, has[0]), (last, has[1])):

        @pl.when(edge & jnp.logical_not(there))
        def _():
            side_recv[...] = jnp.zeros_like(side_recv)

    row_in = iota((lons, lats), 0)
    lane_in = iota((lons, lats), 1)
    keep_w = jnp.where(row_in == 0, 0.0, 1.0).astype(F32)
    keep_e = jnp.where(row_in == lons - 1, 0.0, 1.0).astype(F32)
    keep_s = jnp.where(lane_in == 0, 0.0, 1.0).astype(F32)
    keep_n = jnp.where(lane_in == lats - 1, 0.0, 1.0).astype(F32)
    turns = angles(dirs)

    def advect(f, carry):
        total, courant = carry
        for d, (cos_d, sin_d) in enumerate(turns):
            x = x_ref[f, d]
            a = courant * abs(cos_d)
            b = courant * abs(sin_d)
            if cos_d > 0:
                along = (a * keep_w) * pltpu.roll(x, 1, 0)
            else:
                along = (a * keep_e) * pltpu.roll(x, lons - 1, 0)
            if sin_d > 0:
                across = (b * keep_s) * pltpu.roll(x, 1, 1)
            else:
                across = (b * keep_n) * pltpu.roll(x, lats - 1, 1)
            moved = (1.0 - a - b) * x + along + across
            adv_ref[f, d] = moved
            total = total + moved
        return total, courant * 0.93

    carry = (jnp.zeros((lons, lats), F32), jnp.float32(0.7))
    for i in range(LOADS):
        if i > 0:
            send_halos(i, cuts[1:])
        load(i).wait()
        carry = lax.fori_loop(i * per_load, (i + 1) * per_load, advect, carry)
    total = carry[0]

    local[4].wait()
    local[5].wait()
    blocks, slots = weight_ref.shape[0], weight_ref.shape[1]
    block_of = iota((rows, lats), 1) // rows
    wide, picks = [], []
    for k in range(slots):
        wide.append(jnp.concatenate([weight_ref[b, k] for b in range(blocks)], axis=1))
        pick = jnp.zeros((rows, lats), jnp.int32)
        for b in range(blocks):
            pick = jnp.where(block_of == b, source_ref[k, b], pick)
        picks.append(pick)
    for source in range(blocks):
        part = jnp.zeros((rows, lats), F32)
        for k in range(slots):
            part = part + jnp.where(picks[k] == source, wide[k], 0.0)
        mix_ref[source * rows : (source + 1) * rows, :] = part

    for step in range(1, gy_n):
        lat_arrival(step).wait_recv()
    for edge, there in ((first, has[0]), (last, has[1])):

        @pl.when(edge & there)
        def _():
            for j in range(gy_n):
                side_arrival(j).wait_recv()

    beside = jnp.where(first, 0, jnp.where(last, span - 1, -width))
    from_side = (in_half == beside) | (in_half == beside + span)
    for j in range(gy_n):
        block = jnp.where(from_side, side_recv[j], lat_recv[j])
        lat_ref[j * rows : j * rows + TILE, :] = block
        lat_ref[j * rows + TILE : (j + 1) * rows, :] = pltpu.roll(block, half, 1)
    low_all = lat_ref[...]
    lat_row = iota((lats, width), 0)
    lat_lane = iota((lats, width), 1)
    lower = jnp.where(lat_row == 0, 0.0, pltpu.roll(low_all, 1, 0))
    upper = jnp.where(lat_row == lats - 1, 0.0, pltpu.roll(low_all, lats - 1, 0))
    around = upper + lower + pltpu.roll(low_all, width - 1, 1) + pltpu.roll(low_all, 1, 1) - 4.0 * low_all
    drag_u, drag_v = turned(low_all, 1 - 2 * span), turned(low_all, 1 - span)
    is_u = (lat_lane >= 1) & (lat_lane <= lons)
    is_v = (lat_lane >= span + 1) & (lat_lane <= span + lons)
    low_next = (low_all + 0.2 * around) / jnp.where(is_u, drag_u, jnp.where(is_v, drag_v, 1.0))
    low_v = turned(low_next, -span)
    surface = jnp.sqrt(low_next * low_next + low_v * low_v + 0.25)
    stress = jnp.where(
        lat_lane < lons, turned(surface * low_next, -1),
        jnp.where(lat_lane < 2 * lons, turned(surface * low_v, lons - 1), 0.0),
    )
    wave = lax.dot_general(
        stress, mix_ref[...], (((0,), (0,)), ((), ())),
        precision=lax.Precision.HIGHEST, preferred_element_type=F32,
    )
    wave_x, wave_y = wave[0:lons], wave[lons : 2 * lons]
    for d, (cos_d, sin_d) in enumerate(turns):
        push_ref[d] = jnp.maximum(0.0, wave_x * cos_d + wave_y * sin_d)

    for side in range(2):

        @pl.when(has[side])
        def _():
            col_copy(1 - side).wait_recv()

        @pl.when(jnp.logical_not(has[side]))
        def _():
            col_recv[side] = jnp.zeros((rows, width), F32)

        @pl.when(has[2 + side])
        def _():
            for field in range(2):
                row_copy(field, side == 0).wait_recv()

        @pl.when(jnp.logical_not(has[2 + side]))
        def _():
            row_recv[side] = jnp.zeros_like(row_recv[side])

    for level in range(levels):
        drag = drag_of(level)
        for field, (ref, out) in enumerate(((u_ref, u_out), (v_ref, v_out))):
            x = ref[level]
            slot = field * levels + level
            down = jnp.where(row == 0, row_recv[0, field, level : level + 1, :], pltpu.roll(x, 1, 0))
            up = jnp.where(row == rows - 1, row_recv[1, field, level : level + 1, :], pltpu.roll(x, rows - 1, 0))
            left = jnp.where(lane == 0, pltpu.roll(col_recv[0], (0 - slot) % width, 1), pltpu.roll(x, 1, 1))
            right = jnp.where(
                lane == width - 1, pltpu.roll(col_recv[1], (width - 1 - slot) % width, 1), pltpu.roll(x, width - 1, 1)
            )
            out[level] = (x + 0.2 * (up + down + right + left - 4.0 * x)) / drag

    def turn(count, begin):
        theta = -math.pi / 2 + (iota((count, lats), 0).astype(F32) + (begin + 0.5)) * (2.0 * math.pi / dirs)
        return jnp.abs(jnp.cos(theta))

    turn_w, turn_e = turn(split, 0), turn(dirs - split, split)

    def edges(f, carry):
        acc_w, acc_e, courant = carry
        value_w = (courant * turn_w) * halo_w[f]
        value_e = (courant * turn_e) * halo_e[f]
        edge_w_ref[f] = value_w
        edge_e_ref[f] = value_e
        return acc_w + value_w, acc_e + value_e, courant * 0.93

    sums = (jnp.zeros((split, lats), F32), jnp.zeros((dirs - split, lats), F32), jnp.float32(0.7))
    for i in cuts:
        if i == cuts[-1]:
            for to_east, there in beyond:

                @pl.when(there)
                def _():
                    side_copy(to_east).wait_send()

            for to_east, there in neighbours:

                @pl.when(there)
                def _():
                    for k in cuts[:-1]:
                        halo_copy(to_east, k).wait_send()

            for step in range(1, gy_n):
                lat_copy(step).wait_send()

            for to_upper in (False, True):

                @pl.when(has[3 if to_upper else 2])
                def _():
                    for field in range(2):
                        row_copy(field, to_upper).wait_send()

            for side in range(2):

                @pl.when(has[side])
                def _():
                    col_copy(side).wait_send()

        for to_east, there in arrivals:

            @pl.when(there)
            def _():
                halo_copy(to_east, i).wait_recv()

        sums = lax.fori_loop(begins[i], begins[i] + HALO_CUTS[i], edges, sums)
    sum_w = jnp.sum(sums[0], axis=0, keepdims=True)
    sum_e = jnp.sum(sums[1], axis=0, keepdims=True)
    energy_ref[...] = total + jnp.where(row_in == 0, sum_w, 0.0) + jnp.where(row_in == lons - 1, sum_e, 0.0)
    for to_east, there in neighbours:

        @pl.when(there)
        def _():
            halo_copy(to_east, cuts[-1]).wait_send()


def finish_kernel(
    adv_ref, edge_w_ref, edge_e_ref, energy_ref, push_ref, u_ref, v_ref, mask_ref,
    out_hbm, u_hbm, v_hbm,
    stage, out_sem, wind_sem,
):
    freqs, dirs, lons, lats = stage.shape
    winds = [
        pltpu.make_async_copy(u_ref, u_hbm, wind_sem.at[0]),
        pltpu.make_async_copy(v_ref, v_hbm, wind_sem.at[1]),
    ]
    for copy in winds:
        copy.start()
    split = direction_split(dirs)
    row_in = iota((lons, lats), 0)
    mask = mask_ref[...].astype(F32)
    energy = energy_ref[...] / (0.2 * freqs * dirs)

    def out_copy(f, h):
        part = pl.ds(0, split) if h == 0 else pl.ds(split, dirs - split)
        return pltpu.make_async_copy(stage.at[f, part], out_hbm.at[f, part], out_sem.at[f, h])

    def one(f, carry):
        fraction = f.astype(F32) / (freqs - 1)
        scale = mask / (1.0 + (0.05 + 0.5 * fraction) * energy)
        grow = scale * (0.1 + 0.4 * fraction)
        for d in range(dirs):
            moved = adv_ref[f, d]
            if d < split:
                moved = moved + jnp.where(row_in == 0, edge_w_ref[f, d : d + 1, :], 0.0)
            else:
                moved = moved + jnp.where(row_in == lons - 1, edge_e_ref[f, d - split : d - split + 1, :], 0.0)
            stage[f, d] = moved * (scale + grow * push_ref[d])
            if d == split - 1:
                out_copy(f, 0).start()
        out_copy(f, 1).start()
        return carry

    lax.fori_loop(0, freqs, one, 0)

    def finish(f, carry):
        out_copy(f, 0).wait()
        out_copy(f, 1).wait()
        return carry

    lax.fori_loop(0, freqs, finish, 0)
    for copy in winds:
        copy.wait()


def solution(mesh):
    gx_n, gy_n = mesh.shape["gx"], mesh.shape["gy"]
    vmem = pl.BlockSpec(memory_space=pltpu.VMEM)
    anywhere = pl.BlockSpec(memory_space=pltpu.HBM)

    def per_device(wind_u, wind_v, turbines, rotor_level, block_source, block_weight, spectra, sea_mask):
        freqs, dirs, lons, lats = spectra.shape
        levels, rows, width = wind_u.shape
        split = direction_split(dirs)
        dma = pltpu.SemaphoreType.DMA

        def in_hbm(x):
            return pltpu.with_memory_space_constraint(x, pltpu.HBM)

        handed = pl.pallas_call(
            functools.partial(exchange_kernel, (gx_n, gy_n)),
            out_shape=(
                pltpu.VMEM(spectra.shape, F32),
                pltpu.VMEM((freqs, split, lats), F32),
                pltpu.VMEM((freqs, dirs - split, lats), F32),
                pltpu.VMEM((lons, lats), F32),
                pltpu.VMEM((dirs, lons, lats), F32),
                pltpu.VMEM(wind_u.shape, F32),
                pltpu.VMEM(wind_u.shape, F32),
            ),
            in_specs=[anywhere] * 7,
            out_specs=(vmem,) * 7,
            scratch_shapes=[
                pltpu.VMEM(spectra.shape, F32),
                pltpu.VMEM((freqs, dirs - split, lats), F32),
                pltpu.VMEM((freqs, split, lats), F32),
                pltpu.VMEM((freqs, split, lats), F32),
                pltpu.VMEM((freqs, dirs - split, lats), F32),
                pltpu.VMEM(wind_u.shape, F32),
                pltpu.VMEM(wind_u.shape, F32),
                pltpu.VMEM((rows, width), jnp.int32),
                pltpu.VMEM((rows, width), jnp.int32),
                pltpu.VMEM(block_weight.shape, F32),
                pltpu.SMEM(block_source.shape[::-1], jnp.int32),
                pltpu.VMEM((2, rows, width), F32),
                pltpu.VMEM((2, rows, width), F32),
                pltpu.VMEM((2, 2, levels, width), F32),
                pltpu.VMEM((gy_n, TILE, width), F32),
                pltpu.VMEM((gy_n, TILE, width), F32),
                pltpu.VMEM((2, TILE, width), F32),
                pltpu.VMEM((gy_n, TILE, width), F32),
                pltpu.VMEM((lats, lats), F32),
                pltpu.VMEM((lats, width), F32),
                dma((8,)),
                dma((LOADS,)),
                dma((2, len(HALO_CUTS))),
                dma((2, len(HALO_CUTS))),
                dma((2,)),
                dma((2,)),
                dma((2, 2)),
                dma((2, 2)),
                dma((gy_n - 1,)),
                dma((gy_n - 1,)),
                dma((2,)),
                dma((gy_n,)),
            ],
            compiler_params=pltpu.CompilerParams(
                collective_id=0, has_side_effects=True, vmem_limit_bytes=20 * 2**20
            ),
        )(
            in_hbm(wind_u), in_hbm(wind_v), in_hbm(turbines), in_hbm(rotor_level), in_hbm(block_source.T),
            in_hbm(block_weight), in_hbm(spectra),
        )
        adv, edge_w, edge_e, energy, push, u_next, v_next = handed
        spectra_next, u_done, v_done = pl.pallas_call(
            finish_kernel,
            out_shape=(
                jax.ShapeDtypeStruct(spectra.shape, F32),
                jax.ShapeDtypeStruct(wind_u.shape, F32),
                jax.ShapeDtypeStruct(wind_u.shape, F32),
            ),
            in_specs=[vmem] * 8,
            out_specs=(anywhere,) * 3,
            scratch_shapes=[
                pltpu.VMEM(spectra.shape, F32),
                dma((freqs, 2)),
                dma((2,)),
            ],
            compiler_params=pltpu.CompilerParams(vmem_limit_bytes=20 * 2**20),
        )(adv, edge_w, edge_e, energy, push, u_next, v_next, sea_mask)
        return u_done, v_done, spectra_next

    in_specs = (
        P(None, "gy", "gx"),
        P(None, "gy", "gx"),
        P("gy", "gx"),
        P("gy", "gx"),
        P(),
        P(),
        P(None, None, ("gx", "gy"), None),
        P(("gx", "gy"), None),
    )
    out_specs = (P(None, "gy", "gx"), P(None, "gy", "gx"), P(None, None, ("gx", "gy"), None))
    return jax.shard_map(per_device, mesh=mesh, in_specs=in_specs, out_specs=out_specs, check_vma=False)
```
